512 devices in a mesh: section: 4 (over x), space: 128 (over y, z, core).
Axes of the slice: x: 4, y: 4, z: 16, core: 2. Of those that a mesh axis runs over, the one named last changes fastest.
Arguments:
- feats: bfloat16 [4, 96, 196608], P('section', None, 'space'), may hold values from -6 to 6
- mask: int32 [4, 196608], P('section', 'space'), may hold values 0 or 1
- conv_w: bfloat16 [4, 27, 96, 96], P('section'), may hold values from -0.125 to 0.125
- rules: int32 [4, 384, 26], P('section', 'space'), may hold values from 0 to 5
- send_lists: int32 [4, 128, 2, 1], P('section', 'space'), may hold values from 0 to 2
- pool_map: int32 [4, 384, 8], P('section', 'space'), may hold values from 0 to 3, as said below
- send_order: int32 [4, 128, 1536], P('section', 'space'), may hold values from 0 to 1535, each once within a row
- patch_order: int32 [4, 128, 1536], P('section', 'space'), may hold values from 0 to 1535, each once within a row
- ln_gain: bfloat16 [4, 96], P('section'), may hold values from 0.099609375 to 1.8984375
- w_query: bfloat16 [4, 96, 96], P('section'), may hold values from -5 to 5
- w_key: bfloat16 [4, 96, 96], P('section'), may hold values from -5 to 5
- w_value: bfloat16 [4, 96, 96], P('section'), may hold values from -0.625 to 0.625
- w_out: bfloat16 [4, 96, 96], P('section'), may hold values from -0.625 to 0.625
Outputs:
- result: bfloat16 [4, 96, 196608], P('section', None, 'space')
The draws below stay inside these ranges and needn't reach their ends.
Inputs may be any that keep to these rules, and one draw needn't show every extreme that they name: `pool_map`: in the rows of one space index, each of the numbers 0 to 2 appears exactly once; every other entry is 3, an empty octant.
All inputs are finite; a program needn't handle non-finite values. No bound on the sum of `mask` on one device may be relied on, other than what follows from the above.
Results may differ from the reference program's by a relative error of at most 0.005.
Values may be sent and summed in bfloat16 or wider, within the bound.
No kernel may reach another device: no remote copies, remote signals or barrier semaphores. Data moves between devices by JAX's collectives and lax.ppermute only.
A program may use at most 64 MiB of HBM per device.

```python
import math
import jax
import jax.numpy as jnp
import numpy as np
from jax import lax

C = 96
HEADS = 6
HEAD_DIM = 16
EDGE = 8
PATCH = 384
BLK = 3
SEND = 1
TOK_DEV = 1536
BLOCKS = 384
TOKENS = 196608
N_SECTION = 4
N_SPACE = 128


def draw_pool_map(key, part):
    row_count = N_SECTION * N_SPACE
    slot_count = BLK * 8
    ranks = jnp.arange(slot_count, dtype=jnp.int32)
    entries = jnp.where(ranks < BLK, ranks, BLK).astype(jnp.int32)

    def one_row(row_key):
        ordering = jax.random.permutation(row_key, slot_count)
        return jnp.zeros((slot_count,), jnp.int32).at[ordering].set(entries)
    row_keys = jax.random.split(jax.random.fold_in(key, 21), row_count)
    tables = jax.vmap(one_row)(row_keys)
    return tables.reshape(N_SECTION, N_SPACE * BLK, 8)


def shared_base(key):
    return jax.random.truncated_normal(jax.random.fold_in(key, 11), -4.0, 4.0, (N_SECTION, C, C), jnp.float32)


def draw_w_query(key, part):
    base = shared_base(key)
    return (base / math.sqrt(C)).astype(jnp.bfloat16)


def draw_w_key(key, part):
    fresh = jax.random.truncated_normal(jax.random.fold_in(key, 12), -4.0, 4.0, (N_SECTION, C, C), jnp.float32)
    return (fresh / math.sqrt(C)).astype(jnp.bfloat16)


def with_ends(array, stream_key, smallest, high):
    spot = [jax.random.randint(jax.random.fold_in(stream_key, axis), (), 0, length) for axis, length in enumerate(array.shape)]
    longest = array.shape.index(max(array.shape))
    neighbour = spot[:longest] + [(spot[longest] + 1) % array.shape[longest]] + spot[longest + 1:]
    return array.at[tuple(spot)].set(smallest).at[tuple(neighbour)].set(high)


def block_scale(own_key, extent, shards, least, top_value):
    factor_of, own = 1.0, jax.random.fold_in(own_key, 6)
    for dim, parts in shards:
        draws = jnp.exp(jax.random.uniform(jax.random.fold_in(own, dim), (parts,), jnp.float32, least / len(shards), top_value / len(shards)))
        factor_of = factor_of * jnp.repeat(draws, extent[dim] // parts).reshape([-1 if axis == dim else 1 for axis in range(len(extent))])
    return factor_of


def scatter_about(own_key, shape, spread, most, cuts=(), kind=jnp.bfloat16):
    drawn = jax.random.normal(own_key, shape, jnp.float32) * spread
    if len(cuts) > 0:
        drawn = block_scale(own_key, shape, cuts, -0.22, 0.18) * drawn
    return jnp.clip(drawn, min=-most, max=most).astype(kind)


def setup_inputs(seed: int = 0) -> dict:
    arg_keys = jax.random.split(jax.random.key(seed), 14)
    return {
        "feats": scatter_about(arg_keys[0], (N_SECTION, C, TOKENS), 1.0, 6.0, ((0, 4), (2, 128))),
        "mask": with_ends((jax.random.randint(arg_keys[1], (N_SECTION, TOKENS), 0, 5) < 3).astype(jnp.int32), jax.random.fold_in(arg_keys[1], 1), 0, 1),
        "conv_w": scatter_about(arg_keys[2], (N_SECTION, 27, C, C), (27 * C) ** -0.5, 0.125, ((0, 4),)),
        "rules": with_ends(jax.random.randint(arg_keys[3], (N_SECTION, BLOCKS, 26), 0, BLK + 2 * SEND + 1), jax.random.fold_in(arg_keys[3], 1), 0, BLK + 2 * SEND).astype(jnp.int32),
        "send_lists": with_ends(jax.random.randint(arg_keys[4], (N_SECTION, N_SPACE, 2, SEND), 0, BLK), jax.random.fold_in(arg_keys[4], 1), 0, BLK - 1).astype(jnp.int32),
        "pool_map": draw_pool_map(jax.random.fold_in(arg_keys[13], 71), 0),
        "send_order": jax.vmap(lambda own: jax.random.permutation(own, TOK_DEV))(jax.random.split(arg_keys[6], N_SECTION * N_SPACE)).reshape((N_SECTION, N_SPACE, TOK_DEV)).astype(jnp.int32),
        "patch_order": jax.vmap(lambda own: jax.random.permutation(own, TOK_DEV))(jax.random.split(arg_keys[7], N_SECTION * N_SPACE)).reshape((N_SECTION, N_SPACE, TOK_DEV)).astype(jnp.int32),
        "ln_gain": jnp.clip(1.0 + 0.18 * jax.random.normal(arg_keys[8], (N_SECTION, C), jnp.float32), 0.099609375, 1.8984375).astype(jnp.bfloat16),
        "w_query": draw_w_query(jax.random.fold_in(arg_keys[13], 71), 0),
        "w_key": draw_w_key(jax.random.fold_in(arg_keys[13], 71), 0),
        "w_value": scatter_about(arg_keys[11], (N_SECTION, C, C), C ** -0.5, 0.625, ((0, 4),)),
        "w_out": scatter_about(arg_keys[12], (N_SECTION, C, C), C ** -0.5, 0.625, ((0, 4),)),
    }


EPSILON = 1e-05
MASK_FILL = -1e+30

def offset_tables():
    padded_side = EDGE + 2
    coords = np.arange(padded_side) - 1
    grid_x, grid_y, grid_z = np.meshgrid(coords, coords, coords, indexing='ij')

    def direction(grid):
        return np.where(grid < 0, 0, np.where(grid >= EDGE, 2, 1))
    offset = direction(grid_x) * 9 + direction(grid_y) * 3 + direction(grid_z)
    source = (np.mod(grid_x, EDGE) * EDGE + np.mod(grid_y, EDGE)) * EDGE + np.mod(grid_z, EDGE)
    inner_range = np.arange(EDGE)
    inner_x, inner_y, inner_z = np.meshgrid(inner_range, inner_range, inner_range, indexing='ij')
    view_index = np.stack([(((inner_x + shift_x) * padded_side + inner_y + shift_y) * padded_side + inner_z + shift_z).reshape(-1) for shift_x in range(3) for shift_y in range(3) for shift_z in range(3)])
    half_edge = EDGE // 2
    octant = (inner_x // half_edge * 4 + inner_y // half_edge * 2 + inner_z // half_edge).reshape(-1)
    within = ((inner_x % half_edge * half_edge + inner_y % half_edge) * half_edge + inner_z % half_edge).reshape(-1)
    return (offset.reshape(-1).astype(np.int32), source.reshape(-1).astype(np.int32), view_index.astype(np.int32), octant.astype(np.int32), within.astype(np.int32))

def attend_patch(group_items):
    query, keyed, valued, key_flags = group_items
    scores = jnp.einsum('hdq,hdk->hqk', query.astype(jnp.float32), keyed.astype(jnp.float32)) * (1.0 / np.sqrt(HEAD_DIM))
    visible = (key_flags[None, None, :] > 0) | jnp.eye(PATCH, dtype=bool)[None]
    scores = jnp.where(visible, scores, MASK_FILL)
    row_max = lax.optimization_barrier(jnp.max(scores, axis=-1, keepdims=True))
    exponent = jnp.exp(scores - row_max)
    row_total = lax.optimization_barrier(jnp.sum(exponent, axis=-1, keepdims=True))
    weights = (exponent / row_total).astype(jnp.bfloat16)
    return jnp.einsum('hqk,hdk->hdq', weights.astype(jnp.float32), valued.astype(jnp.float32)).astype(jnp.bfloat16)

def reference(feats, mask, conv_w, rules, send_lists, pool_map, send_order, patch_order, ln_gain, w_query, w_key, w_value, w_out):
    offset, source, view_index, octant, within = offset_tables()
    voxels = EDGE ** 3
    half_edge = EDGE // 2
    coarse = half_edge ** 3
    blocks_all = N_SPACE * BLK
    tokens_all = blocks_all * voxels
    pair_count = TOK_DEV // N_SPACE
    patch_count = tokens_all // PATCH
    block_ids = jnp.arange(blocks_all, dtype=jnp.int32)
    device = block_ids // BLK
    lower_dev = device - 1
    upper_dev = device + 1
    lower_clip = jnp.clip(lower_dev, 0, N_SPACE - 1)
    upper_clip = jnp.clip(upper_dev, 0, N_SPACE - 1)
    outputs = []
    previous = None
    for section in range(N_SECTION):
        active_float = mask[section].astype(jnp.float32)
        masked = feats[section] * mask[section].astype(feats.dtype)
        blocks = masked.reshape(C, blocks_all, voxels)
        block_table = jnp.concatenate([blocks, jnp.zeros((C, 1, voxels), blocks.dtype)], axis=1).reshape(C, -1)
        rule_rows = rules[section]
        neighbor = jnp.concatenate([rule_rows[:, :13], (block_ids % BLK)[:, None], rule_rows[:, 13:]], axis=1).astype(jnp.int32)
        own_global = device[:, None] * BLK + neighbor
        low_slot = send_lists[section][lower_clip[:, None], 1, jnp.clip(neighbor - BLK, 0, SEND - 1)]
        high_slot = send_lists[section][upper_clip[:, None], 0, jnp.clip(neighbor - BLK - SEND, 0, SEND - 1)]
        low_global = jnp.where(lower_dev[:, None] >= 0, lower_dev[:, None] * BLK + low_slot, blocks_all)
        high_global = jnp.where(upper_dev[:, None] < N_SPACE, upper_dev[:, None] * BLK + high_slot, blocks_all)
        global_ids = jnp.where(neighbor < BLK, own_global, jnp.where(neighbor < BLK + SEND, low_global, jnp.where(neighbor < BLK + 2 * SEND, high_global, blocks_all))).astype(jnp.int32)
        gather_index = (global_ids[:, jnp.asarray(offset)] * voxels + jnp.asarray(source)[None, :]).astype(jnp.int32)
        padded = jnp.take(block_table, gather_index.reshape(-1), axis=1).reshape(C, blocks_all, -1)
        conv_sum = jnp.zeros((C, blocks_all, voxels), jnp.float32)
        for position in range(27):
            shifted = jnp.take(padded, jnp.asarray(view_index[position]), axis=2).astype(jnp.float32)
            conv_sum = conv_sum + jnp.einsum('oc,cbv->obv', conv_w[section, position].astype(jnp.float32), shifted)
        conv_out = conv_sum.reshape(C, tokens_all) * active_float[None, :]
        pooled = conv_out.reshape(C, blocks_all, half_edge, 2, half_edge, 2, half_edge, 2).mean(axis=(3, 5, 7)).reshape(C, blocks_all, coarse).astype(jnp.bfloat16)
        if previous is None:
            lifted = jnp.zeros((C, tokens_all), jnp.float32)
        else:
            child_slot = pool_map[section]
            child_global = jnp.where(child_slot < BLK, device[:, None] * BLK + child_slot, blocks_all).astype(jnp.int32)
            child_table = jnp.concatenate([previous, jnp.zeros((C, 1, coarse), previous.dtype)], axis=1).reshape(C, -1)
            lift_index = (child_global[:, jnp.asarray(octant)] * coarse + jnp.asarray(within)[None, :]).astype(jnp.int32)
            lifted = jnp.take(child_table, lift_index.reshape(-1), axis=1).astype(jnp.float32)
        previous = pooled
        hidden = ((masked.astype(jnp.float32) + conv_out + lifted) * active_float[None, :]).astype(jnp.bfloat16)
        owner = jnp.arange(N_SPACE, dtype=jnp.int32)[:, None]
        slot_held = patch_order[section]
        source_dev = slot_held // pair_count
        within_pair = slot_held % pair_count
        token_local = send_order[section][source_dev, owner * pair_count + within_pair]
        serial_source = (source_dev * TOK_DEV + token_local).reshape(-1).astype(jnp.int32)
        serial = hidden[:, serial_source]
        serial_mask = mask[section][serial_source]
        float_values = serial.astype(jnp.float32)
        center = lax.optimization_barrier(jnp.mean(float_values, axis=0, keepdims=True))
        variance = lax.optimization_barrier(jnp.mean((float_values - center) ** 2, axis=0, keepdims=True))
        normed = ((float_values - center) / jnp.sqrt(variance + EPSILON) * ln_gain[section].astype(jnp.float32)[:, None]).astype(jnp.bfloat16)
        query = jnp.dot(w_query[section], normed, preferred_element_type=jnp.float32).astype(jnp.bfloat16)
        keyed = jnp.dot(w_key[section], normed, preferred_element_type=jnp.float32).astype(jnp.bfloat16)
        valued = jnp.dot(w_value[section], normed, preferred_element_type=jnp.float32).astype(jnp.bfloat16)

        def by_patch(tensor):
            return tensor.reshape(HEADS, HEAD_DIM, patch_count, PATCH).transpose(2, 0, 1, 3)
        attended = lax.map(attend_patch, (by_patch(query), by_patch(keyed), by_patch(valued), serial_mask.reshape(patch_count, PATCH)))
        attended = attended.transpose(1, 2, 0, 3).reshape(C, tokens_all)
        projected = jnp.dot(w_out[section], attended, preferred_element_type=jnp.float32)
        finished = ((serial.astype(jnp.float32) + projected) * serial_mask.astype(jnp.float32)[None, :]).astype(jnp.bfloat16)
        outputs.append(jnp.zeros((C, tokens_all), finished.dtype).at[:, serial_source].set(finished))
    return jnp.stack(outputs)
```

```python
import math

import jax
import jax.numpy as jnp
from jax import lax
from jax.experimental import pallas as pl
from jax.experimental.pallas import tpu as pltpu
from jax.sharding import PartitionSpec as P

HEADS = 6
HEAD_DIM = 16
EDGE = 8
PATCH = 384
EPSILON = 1e-05
MASK_FILL = -1e30
LANES = 128
VOX = EDGE**3
ROWS = 10


def shifted(block, axis, distance):
    devices = range(lax.axis_size(axis))
    route = [(i - distance, i) for i in devices if i - distance in devices]
    return lax.ppermute(block, axis, route)


def vmem():
    return pl.BlockSpec(memory_space=pltpu.VMEM)


def smem():
    return pl.BlockSpec(memory_space=pltpu.SMEM)


def lane_of(shape):
    return lax.broadcasted_iota(jnp.int32, shape, len(shape) - 1)


def copy_rows(count, read_index, write_index, src, dst):
    step = 16

    def body(outer, carry):
        base = outer * step
        for inner in range(step):
            i = base + inner
            dst[pl.ds(write_index(i), 1), :] = src[pl.ds(read_index(i), 1), :]
        return carry

    lax.fori_loop(0, count // step, body, 0)


def pack_rows(slots, packed, with_mask):
    peers = slots.shape[0] // 12
    lane = lane_of((peers, LANES))
    tokens = [slots[t * peers : (t + 1) * peers, :] for t in range(12)]
    for group in range(3):
        extra = tokens[4 * group + 3]
        for j in range(3):
            row = jnp.where(
                lane < 96, tokens[4 * group + j], pltpu.roll(extra, 96 - 32 * j, axis=1)
            )
            packed[pl.ds(3 * group + j, peers, stride=ROWS), :] = row
    last = jnp.zeros((peers, LANES), jnp.float32)
    if with_mask:
        for t in range(12):
            last = jnp.where(lane == t, pltpu.roll(tokens[t], 32 + t, axis=1), last)
    packed[pl.ds(ROWS - 1, peers, stride=ROWS), :] = last


def unpack_rows(packed, slots, with_mask):
    peers = slots.shape[0] // 12
    lane = lane_of((peers, LANES))
    if with_mask:
        flags = packed[pl.ds(ROWS - 1, peers, stride=ROWS), :]
    for group in range(3):
        rows = [packed[pl.ds(3 * group + j, peers, stride=ROWS), :] for j in range(3)]
        extra = jnp.zeros((peers, LANES), jnp.float32)
        for j in range(3):
            spot = (lane >= 32 * j) & (lane < 32 * j + 32)
            extra = jnp.where(spot, pltpu.roll(rows[j], (32 * j + 32) % LANES, axis=1), extra)
        for j in range(4):
            t = 4 * group + j
            value = rows[j] if j < 3 else extra
            value = jnp.where(lane < 96, value, 0.0)
            if with_mask:
                value = jnp.where(lane == 96, pltpu.roll(flags, 96 - t, axis=1), value)
            slots[t * peers : (t + 1) * peers, :] = value


def layout_kernel(feats, mask, table):
    tokens = feats.shape[1]
    flags = mask[...].astype(jnp.float32)
    values = feats[...].astype(jnp.float32) * flags
    row = lax.broadcasted_iota(jnp.int32, (LANES - 96, tokens), 0)
    tail = jnp.where(row == 0, jnp.broadcast_to(flags, row.shape), 0.0)
    table[...] = jnp.concatenate([values, tail], axis=0).T


def conv_kernel(rules, own, low, high, weights, joined, pooled, table, padded, views, halves):
    blocks = own.shape[0] // VOX
    pad_lanes = jnp.zeros((LANES - 96, VOX), jnp.float32)
    for b in range(blocks):
        table[b] = own[b * VOX : (b + 1) * VOX, :].reshape(EDGE, EDGE, EDGE, LANES)
    for spot, ref in ((blocks, low), (blocks + 1, high)):
        values = jnp.concatenate([ref[...].astype(jnp.float32), pad_lanes], axis=0).T
        table[spot] = values.reshape(EDGE, EDGE, EDGE, LANES)
    table[blocks + 2] = jnp.zeros((EDGE, EDGE, EDGE, LANES), jnp.float32)

    def span(direction):
        if direction < 0:
            return pl.ds(EDGE - 1, 1), pl.ds(0, 1)
        if direction > 0:
            return pl.ds(0, 1), pl.ds(EDGE + 1, 1)
        return pl.ds(0, EDGE), pl.ds(1, EDGE)

    for b in range(blocks):

        def neighbor(dx, dy, dz):
            k = 9 * (dx + 1) + 3 * (dy + 1) + dz + 1
            if k == 13:
                return b
            return rules[b, k if k < 13 else k - 1]

        for dx in (-1, 0, 1):
            sx, tx = span(dx)
            for dy in (-1, 0, 1):
                sy, ty = span(dy)
                here = table[neighbor(dx, dy, 0), sx, sy, :, :]
                below = table[neighbor(dx, dy, -1), sx, sy, :, :]
                above = table[neighbor(dx, dy, 1), sx, sy, :, :]
                z = lax.broadcasted_iota(jnp.int32, here.shape, 2)
                shape = here.shape
                flat = (shape[0] * shape[1] * EDGE, LANES)
                lower = jnp.where(z == EDGE - 1, below, here)
                upper = jnp.where(z == 0, above, here)
                padded[0, tx, ty, :, :] = pltpu.roll(lower, 1, axis=2)
                padded[1, tx, ty, :, :] = here
                padded[2, tx, ty, :, :] = pltpu.roll(upper, EDGE - 1, axis=2)
        for dy in range(3):
            for dz in range(3):
                k = dy * 3 + dz
                window = padded[dz, :, dy : dy + EDGE, :, :]
                views[:, k * LANES : (k + 1) * LANES] = window.reshape(
                    (EDGE + 2) * EDGE * EDGE, LANES
                ).astype(jnp.bfloat16)
        total = jnp.zeros((VOX, LANES), jnp.float32)
        for dx in range(3):
            total = total + jnp.dot(
                views[dx * 64 : dx * 64 + VOX, :], weights[dx], preferred_element_type=jnp.float32
            )
        rows = own[b * VOX : (b + 1) * VOX, :]
        conv = total * rows[:, 96:97]
        joined[b * VOX : (b + 1) * VOX, :] = rows + conv
        quads = conv.reshape(4, 2, 4, 2, EDGE, LANES)
        summed = (quads[:, 0, :, 0] + quads[:, 0, :, 1]) + (quads[:, 1, :, 0] + quads[:, 1, :, 1])
        halves[...] = summed.reshape(16 * EDGE, LANES)
        even = halves[pl.ds(0, 64, stride=2), :]
        odd = halves[pl.ds(1, 64, stride=2), :]
        pooled[b * 64 : (b + 1) * 64, :] = ((even + odd) * 0.125).astype(jnp.bfloat16)


def join_kernel(
    octants, order, joined, coarser, hidden, message, wide, children, rows, slots, packed
):
    blocks = joined.shape[0] // VOX
    wide[...] = coarser[...].astype(jnp.float32)
    count = blocks * 16
    for k in range(4):
        value = wide[pl.ds(k, count, stride=4), :]
        children[pl.ds(k, count, stride=8), :] = value
        children[pl.ds(k + 4, count, stride=8), :] = value
    children[count * 8 : count * 8 + 128, :] = jnp.zeros((128, LANES), jnp.float32)
    z = lax.broadcasted_iota(jnp.int32, (4, 4, EDGE, LANES), 2)
    lane = lax.broadcasted_iota(jnp.int32, (VOX, LANES), 1)
    for b in range(blocks):
        halves = []
        for ox in range(2):
            parts = []
            for oy in range(2):
                near = children[pl.ds(octants[b, 4 * ox + 2 * oy] * 128, 128), :]
                far = children[pl.ds(octants[b, 4 * ox + 2 * oy + 1] * 128, 128), :]
                near = near.reshape(4, 4, EDGE, LANES)
                far = far.reshape(4, 4, EDGE, LANES)
                parts.append(jnp.where(z < 4, near, far))
            halves.append(jnp.concatenate(parts, axis=1))
        lifted = jnp.concatenate(halves, axis=0).reshape(VOX, LANES)
        here = joined[b * VOX : (b + 1) * VOX, :]
        flags = here[:, 96:97]
        value = jnp.where(lane < 96, (here + lifted) * flags, here)
        short = value.astype(jnp.bfloat16)
        hidden[b * VOX : (b + 1) * VOX, :] = short
        rows[b * VOX : (b + 1) * VOX, :] = short.astype(jnp.float32)
    copy_rows(rows.shape[0], lambda i: order[i], lambda i: i, rows, slots)
    pack_rows(slots, packed, True)
    message[...] = packed[...].astype(jnp.bfloat16)


def attend_kernel(
    order, inbound, gain, w_query, w_key, w_value, outbound,
    packed, slots, rows, scores, keys, attended,
):
    packed[...] = inbound[...].astype(jnp.float32)
    unpack_rows(packed, slots, True)
    copy_rows(rows.shape[0], lambda i: order[i], lambda i: i, slots, rows)
    lane = lane_of((PATCH, LANES))
    inside = lane < 96
    row = lax.broadcasted_iota(jnp.int32, (PATCH, PATCH), 0)
    own = row == lax.broadcasted_iota(jnp.int32, (PATCH, PATCH), 1)
    contract = (((1,), (1,)), ((), ()))
    for patch in range(rows.shape[0] // PATCH):
        serial = rows[patch * PATCH : (patch + 1) * PATCH, :]
        flags = serial[:, 96:97]
        values = jnp.where(inside, serial, 0.0)
        center = jnp.sum(values, axis=1, keepdims=True) * (1.0 / 96)
        spread = jnp.where(inside, values - center, 0.0)
        variance = jnp.sum(spread * spread, axis=1, keepdims=True) * (1.0 / 96)
        normed = (spread * lax.rsqrt(variance + EPSILON) * gain[...]).astype(jnp.bfloat16)
        query = lax.dot_general(w_query[...], normed, contract, preferred_element_type=jnp.float32)
        query = (query * (1.0 / math.sqrt(HEAD_DIM))).astype(jnp.bfloat16)
        keyed = lax.dot_general(normed, w_key[...], contract, preferred_element_type=jnp.float32)
        valued = lax.dot_general(w_value[...], normed, contract, preferred_element_type=jnp.float32)
        valued = valued.astype(jnp.bfloat16)
        for head in range(HEADS):
            spot = (lane >= head * HEAD_DIM) & (lane < (head + 1) * HEAD_DIM)
            keys[head * PATCH : (head + 1) * PATCH, :] = jnp.where(spot, keyed, 0.0).astype(
                jnp.bfloat16
            )
        scores[...] = jnp.dot(keys[...], query, preferred_element_type=jnp.float32)
        bias = jnp.where((flags > 0) | own, 0.0, MASK_FILL)
        ones = jnp.ones((HEAD_DIM, PATCH), jnp.bfloat16)
        for head in range(HEADS):
            here = scores[head * PATCH : (head + 1) * PATCH, :] + bias
            top = jnp.max(here, axis=0, keepdims=True)
            exponent = jnp.exp(here - top).astype(jnp.bfloat16)
            left = jnp.concatenate(
                [valued[head * HEAD_DIM : (head + 1) * HEAD_DIM, :], ones], axis=0
            )
            mixed = jnp.dot(left, exponent, preferred_element_type=jnp.float32)
            attended[head * HEAD_DIM : (head + 1) * HEAD_DIM, :] = (
                mixed[:HEAD_DIM] / mixed[HEAD_DIM : HEAD_DIM + 1]
            )
        rows[patch * PATCH : (patch + 1) * PATCH, :] = attended[...].T
    copy_rows(rows.shape[0], lambda i: i, lambda i: order[i], rows, slots)
    pack_rows(slots, packed, False)
    outbound[...] = packed[...].astype(jnp.bfloat16)


def finish_kernel(order, returned, hidden, mask, w_out, result, packed, slots, rows):
    packed[...] = returned[...].astype(jnp.float32)
    unpack_rows(packed, slots, False)
    copy_rows(rows.shape[0], lambda i: i, lambda i: order[i], slots, rows)
    projected = lax.dot_general(
        w_out[...],
        rows[...].astype(jnp.bfloat16),
        (((1,), (1,)), ((), ())),
        preferred_element_type=jnp.float32,
    )
    value = hidden[...].astype(jnp.float32) + projected
    result[...] = (value * mask[...].astype(jnp.float32)).astype(jnp.bfloat16)


def exchange(packed):
    spaces = lax.axis_size("space")
    tiles = packed.reshape(packed.shape[0] // 2, 2, LANES)
    return lax.all_to_all(tiles, "space", split_axis=0, concat_axis=0, tiled=True).reshape(
        packed.shape
    )


def shards(
    feats,
    mask,
    conv_w,
    rules,
    send_lists,
    pool_map,
    send_order,
    patch_order,
    ln_gain,
    w_query,
    w_key,
    w_value,
    w_out,
):
    f32, bf16 = jnp.float32, jnp.bfloat16
    tokens = feats.shape[2]
    blocks = tokens // VOX
    spaces = lax.axis_size("space")
    pair = tokens // spaces
    packed_rows = spaces * ROWS

    def boundary(row_index):
        start = send_lists[0, 0, row_index, 0] * VOX
        piece = lax.dynamic_slice(feats[0], (0, start), (96, VOX))
        flags = lax.dynamic_slice(mask, (0, start), (1, VOX))
        return piece * flags.astype(bf16)

    low = shifted(boundary(1), "space", 1)
    high = shifted(boundary(0), "space", -1)
    table = pl.pallas_call(
        layout_kernel,
        out_shape=jax.ShapeDtypeStruct((tokens, LANES), f32),
        in_specs=[vmem()] * 2,
        out_specs=vmem(),
        name="layout",
    )(feats[0], mask)
    weights = jnp.pad(conv_w[0].transpose(0, 2, 1), ((0, 0), (0, LANES - 96), (0, LANES - 96)))
    weights = weights.reshape(3, 9 * LANES, LANES)
    joined, pooled = pl.pallas_call(
        conv_kernel,
        out_shape=(
            jax.ShapeDtypeStruct((tokens, LANES), f32),
            jax.ShapeDtypeStruct((blocks * 64, LANES), bf16),
        ),
        in_specs=[smem()] + [vmem()] * 4,
        out_specs=(vmem(), vmem()),
        scratch_shapes=[
            pltpu.VMEM((blocks + 3, EDGE, EDGE, EDGE, LANES), f32),
            pltpu.VMEM((3, EDGE + 2, EDGE + 2, EDGE, LANES), f32),
            pltpu.VMEM(((EDGE + 2) * EDGE * EDGE, 9 * LANES), bf16),
            pltpu.VMEM((16 * EDGE, LANES), f32),
        ],
        name="conv",
    )(rules[0], table, low, high, weights)
    coarser = shifted(pooled, "section", 1)
    order_out = send_order[0, 0].reshape(spaces, pair).T.reshape(-1)
    held = patch_order[0, 0]
    order_in = (held % pair) * spaces + held // pair
    hidden, message = pl.pallas_call(
        join_kernel,
        out_shape=(
            jax.ShapeDtypeStruct((tokens, LANES), bf16),
            jax.ShapeDtypeStruct((packed_rows, LANES), bf16),
        ),
        in_specs=[smem()] * 2 + [vmem()] * 2,
        out_specs=(vmem(), vmem()),
        scratch_shapes=[
            pltpu.VMEM((blocks * 64, LANES), f32),
            pltpu.VMEM(((blocks + 1) * 128, LANES), f32),
            pltpu.VMEM((tokens, LANES), f32),
            pltpu.VMEM((tokens, LANES), f32),
            pltpu.VMEM((packed_rows, LANES), f32),
        ],
        name="join",
    )(pool_map[0], order_out, joined, coarser)
    inbound = exchange(message)

    def square(weight):
        return jnp.pad(weight[0], ((0, LANES - 96), (0, LANES - 96)))

    outbound = pl.pallas_call(
        attend_kernel,
        out_shape=jax.ShapeDtypeStruct((packed_rows, LANES), bf16),
        in_specs=[smem()] + [vmem()] * 5,
        out_specs=vmem(),
        scratch_shapes=[
            pltpu.VMEM((packed_rows, LANES), f32),
            pltpu.VMEM((tokens, LANES), f32),
            pltpu.VMEM((tokens, LANES), f32),
            pltpu.VMEM((HEADS * PATCH, PATCH), f32),
            pltpu.VMEM((HEADS * PATCH, LANES), bf16),
            pltpu.VMEM((LANES, PATCH), f32),
        ],
        name="attend",
    )(
        order_in,
        inbound,
        jnp.pad(ln_gain.astype(f32), ((0, 0), (0, LANES - 96))),
        square(w_query),
        square(w_key),
        square(w_value),
    )
    returned = exchange(outbound)
    result = pl.pallas_call(
        finish_kernel,
        out_shape=jax.ShapeDtypeStruct((96, tokens), bf16),
        in_specs=[smem()] + [vmem()] * 4,
        out_specs=vmem(),
        scratch_shapes=[
            pltpu.VMEM((packed_rows, LANES), f32),
            pltpu.VMEM((tokens, LANES), f32),
            pltpu.VMEM((tokens, LANES), f32),
        ],
        name="finish",
    )(
        order_out,
        returned,
        hidden[:, :96].T,
        mask,
        jnp.pad(w_out[0], ((0, 0), (0, LANES - 96))),
    )
    return result[None]


def solution(mesh):
    placed = (
        P("section", None, "space"),
        P("section", "space"),
        P("section", None, None, None),
        P("section", "space", None),
        P("section", "space", None, None),
        P("section", "space", None),
        P("section", "space", None),
        P("section", "space", None),
        P("section", None),
        P("section", None, None),
        P("section", None, None),
        P("section", None, None),
        P("section", None, None),
    )
    return jax.shard_map(
        shards, mesh=mesh, in_specs=placed, out_specs=P("section", None, "space"), check_vma=False
    )
```

```python
import math

import jax
import jax.numpy as jnp
from jax import lax
from jax.experimental import pallas as pl
from jax.experimental.pallas import tpu as pltpu
from jax.sharding import PartitionSpec as P

HEADS = 6
HEAD_DIM = 16
EDGE = 8
PATCH = 384
EPSILON = 1e-05
MASK_FILL = -1e30
LANES = 128
VOX = EDGE**3
ROWS = 10
CONTRACT_LAST = (((1,), (1,)), ((), ()))
VMEM_LIMIT = 24 << 20


def shifted(block, axis, distance):
    devices = range(lax.axis_size(axis))
    route = [(i - distance, i) for i in devices if i - distance in devices]
    return lax.ppermute(block, axis, route)


def vmem():
    return pl.BlockSpec(memory_space=pltpu.VMEM)


def smem():
    return pl.BlockSpec(memory_space=pltpu.SMEM)


def lane_of(shape):
    return lax.broadcasted_iota(jnp.int32, shape, len(shape) - 1)


def copy_rows(count, read_index, write_index, src, dst):
    step = 16

    def body(outer, carry):
        base = outer * step
        for inner in range(step):
            i = base + inner
            dst[pl.ds(write_index(i), 1), :] = src[pl.ds(read_index(i), 1), :]
        return carry

    lax.fori_loop(0, count // step, body, 0)


def pack_rows(slots, packed, with_mask):
    peers = slots.shape[0] // 12
    lane = lane_of((peers, LANES))
    tokens = [slots[t * peers : (t + 1) * peers, :] for t in range(12)]
    for group in range(3):
        extra = tokens[4 * group + 3]
        for j in range(3):
            row = jnp.where(
                lane < 96, tokens[4 * group + j], pltpu.roll(extra, 96 - 32 * j, axis=1)
            )
            packed[pl.ds(3 * group + j, peers, stride=ROWS), :] = row
    last = jnp.zeros((peers, LANES), jnp.float32)
    if with_mask:
        for t in range(12):
            last = jnp.where(lane == t, pltpu.roll(tokens[t], 32 + t, axis=1), last)
    packed[pl.ds(ROWS - 1, peers, stride=ROWS), :] = last


def unpack_rows(packed, slots, with_mask):
    peers = slots.shape[0] // 12
    lane = lane_of((peers, LANES))
    if with_mask:
        flags = packed[pl.ds(ROWS - 1, peers, stride=ROWS), :]
    for group in range(3):
        rows = [packed[pl.ds(3 * group + j, peers, stride=ROWS), :] for j in range(3)]
        extra = jnp.zeros((peers, LANES), jnp.float32)
        for j in range(3):
            spot = (lane >= 32 * j) & (lane < 32 * j + 32)
            extra = jnp.where(spot, pltpu.roll(rows[j], (32 * j + 32) % LANES, axis=1), extra)
        for j in range(4):
            t = 4 * group + j
            value = rows[j] if j < 3 else extra
            value = jnp.where(lane < 96, value, 0.0)
            if with_mask:
                value = jnp.where(lane == 96, pltpu.roll(flags, 96 - t, axis=1), value)
            slots[t * peers : (t + 1) * peers, :] = value


def send_kernel(lists, feats, mask, to_upper, to_lower):
    for out, row_index in ((to_upper, 1), (to_lower, 0)):
        here = pl.ds(pl.multiple_of(lists[row_index] * VOX, VOX), VOX)
        flags = mask[:, here].astype(jnp.float32)
        out[...] = (feats[:, here].astype(jnp.float32) * flags).astype(jnp.bfloat16)


def layout_kernel(octants, feats, mask, taps, table, weights):
    tokens = feats.shape[1]
    flags = mask[...].astype(jnp.float32)
    values = feats[...].astype(jnp.float32) * flags
    token = lax.broadcasted_iota(jnp.int32, (1, tokens), 1)
    x, y, z = (token >> 6) & 7, (token >> 3) & 7, token & 7
    octant = ((token >> 9) << 3) + ((x >> 2) << 2) + ((y >> 2) << 1) + (z >> 2)
    slot = jnp.full((1, tokens), 3, jnp.int32)
    for k in range(octants.shape[0]):
        slot = jnp.where(octant == k, octants[k], slot)
    within = ((x & 3) << 4) + ((y & 3) << 2) + (z & 3)
    child = jnp.where((slot < 3) & (mask[...] > 0), slot * 64 + within, 255).astype(jnp.float32)
    row = lax.broadcasted_iota(jnp.int32, (LANES - 96, tokens), 0)
    tail = jnp.where(row == 0, flags, jnp.where(row == 1, child, 0.0))
    table[...] = jnp.concatenate([values, tail], axis=0).T
    weights[...] = jnp.zeros(weights.shape, jnp.bfloat16)
    for k in range(27):
        at = (k % 9) * LANES
        weights[k // 9, 0:96, at : at + 96] = taps[k]


def conv_kernel(rules, own, low, high, weights, joined, pooled, table, padded, views, halves):
    blocks = own.shape[0] // VOX
    pad_lanes = jnp.zeros((LANES - 96, VOX), jnp.float32)
    for b in range(blocks):
        table[b] = own[b * VOX : (b + 1) * VOX, :].reshape(EDGE, EDGE, EDGE, LANES)
    for spot, ref in ((blocks, low), (blocks + 1, high)):
        values = jnp.concatenate([ref[...].astype(jnp.float32), pad_lanes], axis=0).T
        table[spot] = values.reshape(EDGE, EDGE, EDGE, LANES)
    table[blocks + 2] = jnp.zeros((EDGE, EDGE, EDGE, LANES), jnp.float32)

    def span(direction):
        if direction < 0:
            return pl.ds(EDGE - 1, 1), pl.ds(0, 1)
        if direction > 0:
            return pl.ds(0, 1), pl.ds(EDGE + 1, 1)
        return pl.ds(0, EDGE), pl.ds(1, EDGE)

    for b in range(blocks):

        def neighbor(dx, dy, dz):
            k = 9 * (dx + 1) + 3 * (dy + 1) + dz + 1
            if k == 13:
                return b
            return rules[b, k if k < 13 else k - 1]

        for dx in (-1, 0, 1):
            sx, tx = span(dx)
            for dy in (-1, 0, 1):
                sy, ty = span(dy)
                here = table[neighbor(dx, dy, 0), sx, sy, :, :]
                below = table[neighbor(dx, dy, -1), sx, sy, :, :]
                above = table[neighbor(dx, dy, 1), sx, sy, :, :]
                z = lax.broadcasted_iota(jnp.int32, here.shape, 2)
                shape = here.shape
                flat = (shape[0] * shape[1] * EDGE, LANES)
                lower = jnp.where(z == EDGE - 1, below, here)
                upper = jnp.where(z == 0, above, here)
                padded[0, tx, ty, :, :] = pltpu.roll(lower, 1, axis=2)
                padded[1, tx, ty, :, :] = here
                padded[2, tx, ty, :, :] = pltpu.roll(upper, EDGE - 1, axis=2)
        for dy in range(3):
            for dz in range(3):
                k = dy * 3 + dz
                window = padded[dz, :, dy : dy + EDGE, :, :]
                views[:, k * LANES : (k + 1) * LANES] = window.reshape(
                    (EDGE + 2) * EDGE * EDGE, LANES
                ).astype(jnp.bfloat16)
        total = jnp.zeros((VOX, LANES), jnp.float32)
        for dx in range(3):
            total = total + lax.dot_general(
                views[dx * 64 : dx * 64 + VOX, :],
                weights[dx],
                CONTRACT_LAST,
                preferred_element_type=jnp.float32,
            )
        rows = own[b * VOX : (b + 1) * VOX, :]
        conv = total * rows[:, 96:97]
        joined[b * VOX : (b + 1) * VOX, :] = rows + conv
        quads = conv.reshape(4, 2, 4, 2, EDGE, LANES)
        summed = (quads[:, 0, :, 0] + quads[:, 0, :, 1]) + (quads[:, 1, :, 0] + quads[:, 1, :, 1])
        halves[...] = summed.reshape(16 * EDGE, LANES)
        even = halves[pl.ds(0, 64, stride=2), :]
        odd = halves[pl.ds(1, 64, stride=2), :]
        pooled[b * 64 : (b + 1) * 64, :] = ((even + odd) * 0.125).astype(jnp.bfloat16)


def child_matrix(rows):
    count = rows.shape[0]
    column = lax.broadcasted_iota(jnp.int32, (count, 2 * LANES), 1).astype(jnp.float32)
    return jnp.where(column == rows[:, 97:98], 1.0, 0.0).astype(jnp.bfloat16)


def lift(rows, chosen, coarser):
    blank = jnp.zeros((2 * LANES - coarser.shape[0], LANES), jnp.bfloat16)
    below = jnp.concatenate([coarser, blank], axis=0)
    return rows + jnp.dot(chosen, below, preferred_element_type=jnp.float32)


def gather_kernel(order, joined, slots, chosen):
    copy_rows(slots.shape[0], lambda i: order[i], lambda i: i, joined, slots)
    chosen[...] = child_matrix(slots[...])


def join_kernel(slots, chosen, coarser, message, lifted, packed):
    lifted[...] = lift(slots[...], chosen[...], coarser[...])
    pack_rows(lifted, packed, True)
    message[...] = packed[...].astype(jnp.bfloat16)


def residual_kernel(joined, coarser, hidden):
    blocks = joined.shape[0] // VOX
    for b in range(blocks):
        rows = joined[b * VOX : (b + 1) * VOX, :]
        value = lift(rows, child_matrix(rows), coarser[...])
        hidden[:, b * VOX : (b + 1) * VOX] = value.T[:96].astype(jnp.bfloat16)


def attend_kernel(
    order, inbound, gain, w_query, w_key, w_value, outbound,
    packed, slots, rows, keys, scores, exponents, diagonal, attended,
):
    packed[...] = inbound[...].astype(jnp.float32)
    unpack_rows(packed, slots, True)
    copy_rows(rows.shape[0], lambda i: order[i], lambda i: i, slots, rows)
    lane = lane_of((1, LANES))
    inside = lane < 96
    channel = lax.broadcasted_iota(jnp.int32, (LANES, PATCH), 0)
    factor = math.log2(math.e) / math.sqrt(HEAD_DIM)
    ones = jnp.ones((HEAD_DIM, PATCH), jnp.bfloat16)

    def project(left, right):
        return lax.dot_general(left, right, CONTRACT_LAST, preferred_element_type=jnp.float32)

    for patch in range(rows.shape[0] // PATCH):
        side = patch % 2
        serial = rows[patch * PATCH : (patch + 1) * PATCH, :]
        flags = serial[:, 96:97]
        values = jnp.where(inside, serial, 0.0)
        center = jnp.sum(values, axis=1, keepdims=True) * (1.0 / 96)
        spread = jnp.where(inside, values - center, 0.0)
        variance = jnp.sum(spread * spread, axis=1, keepdims=True) * (1.0 / 96)
        normed = (spread * lax.rsqrt(variance + EPSILON) * gain[...]).astype(jnp.bfloat16)
        query = project(w_query[...], normed) * factor
        query = jnp.where(channel == 96, 1.0, query).astype(jnp.bfloat16)
        keyed = project(normed, w_key[...])
        keyed = jnp.where(lane == 96, jnp.where(flags > 0, 0.0, MASK_FILL), keyed)
        keyed = keyed.astype(jnp.bfloat16)
        keyed_across = project(w_key[...], normed).astype(jnp.bfloat16)
        valued = project(w_value[...], normed).astype(jnp.bfloat16)
        products = query.astype(jnp.float32) * keyed_across.astype(jnp.float32)
        for head in range(HEADS):
            spot = (lane >= head * HEAD_DIM) & (lane < (head + 1) * HEAD_DIM) | (lane == 96)
            keys[side, head * PATCH : (head + 1) * PATCH, :] = keyed * jnp.where(
                spot, 1.0, 0.0
            ).astype(jnp.bfloat16)
        scores[side] = jnp.dot(keys[side], query, preferred_element_type=jnp.float32)
        alone = 1.0 - jnp.broadcast_to(flags, (PATCH, LANES)).T[0:1, :]
        for head in range(HEADS):
            group = slice(head * PATCH, (head + 1) * PATCH)
            channels = slice(head * HEAD_DIM, (head + 1) * HEAD_DIM)
            own = jnp.sum(products[channels], axis=0, keepdims=True)
            for part in range(PATCH // LANES):
                columns = slice(part * LANES, (part + 1) * LANES)
                here = scores[side, group, columns]
                top = jnp.maximum(jnp.max(here, axis=0, keepdims=True), own[:, columns])
                exponents[side, group, columns] = jnp.exp2(here - top).astype(jnp.bfloat16)
                extra = jnp.exp2(own[:, columns] - top) * alone[:, columns]
                diagonal[side, head : head + 1, columns] = extra
            left = jnp.concatenate([valued[channels], ones], axis=0)
            mixed = jnp.dot(left, exponents[side, group, :], preferred_element_type=jnp.float32)
            extra = diagonal[side, head : head + 1, :]
            upper = mixed[:HEAD_DIM] + extra * valued[channels].astype(jnp.float32)
            attended[side, channels, :] = upper / (mixed[HEAD_DIM : HEAD_DIM + 1] + extra)
        rows[patch * PATCH : (patch + 1) * PATCH, :] = attended[side].T
    copy_rows(rows.shape[0], lambda i: i, lambda i: order[i], rows, slots)
    pack_rows(slots, packed, False)
    outbound[...] = packed[...].astype(jnp.bfloat16)


def finish_kernel(order, returned, hidden, mask, w_out, result, packed, slots, rows):
    packed[...] = returned[...].astype(jnp.float32)
    unpack_rows(packed, slots, False)
    copy_rows(rows.shape[0], lambda i: i, lambda i: order[i], slots, rows)
    projected = lax.dot_general(
        w_out[...],
        rows[...].astype(jnp.bfloat16),
        (((1,), (1,)), ((), ())),
        preferred_element_type=jnp.float32,
    )
    value = hidden[...].astype(jnp.float32) + projected
    result[...] = (value * mask[...].astype(jnp.float32)).astype(jnp.bfloat16)


def call(body, outputs, in_specs, scratch=(), name=None):
    return pl.pallas_call(
        body,
        out_shape=outputs,
        in_specs=in_specs,
        out_specs=tuple(vmem() for _ in outputs),
        scratch_shapes=list(scratch),
        compiler_params=pltpu.CompilerParams(vmem_limit_bytes=VMEM_LIMIT),
        name=name,
    )


def exchange(packed):
    spaces = lax.axis_size("space")
    tiles = packed.reshape(packed.shape[0] // 2, 2, LANES)
    return lax.all_to_all(tiles, "space", split_axis=0, concat_axis=0, tiled=True).reshape(
        packed.shape
    )


def shards(
    feats,
    mask,
    conv_w,
    rules,
    send_lists,
    pool_map,
    send_order,
    patch_order,
    ln_gain,
    w_query,
    w_key,
    w_value,
    w_out,
):
    f32, bf16 = jnp.float32, jnp.bfloat16
    tokens = feats.shape[2]
    blocks = tokens // VOX
    spaces = lax.axis_size("space")
    pair = tokens // spaces
    packed_rows = spaces * ROWS

    to_upper, to_lower = call(
        send_kernel,
        (jax.ShapeDtypeStruct((96, VOX), bf16),) * 2,
        [smem()] + [vmem()] * 2,
        name="send",
    )(send_lists.reshape(2), feats[0], mask)
    low = shifted(to_upper, "space", 1)
    high = shifted(to_lower, "space", -1)
    table, weights = call(
        layout_kernel,
        (
            jax.ShapeDtypeStruct((tokens, LANES), f32),
            jax.ShapeDtypeStruct((3, LANES, 9 * LANES), bf16),
        ),
        [smem()] + [vmem()] * 3,
        name="layout",
    )(pool_map.reshape(-1), feats[0], mask, conv_w[0])
    joined, pooled = call(
        conv_kernel,
        (
            jax.ShapeDtypeStruct((tokens, LANES), f32),
            jax.ShapeDtypeStruct((blocks * 64, LANES), bf16),
        ),
        [smem()] + [vmem()] * 4,
        [
            pltpu.VMEM((blocks + 3, EDGE, EDGE, EDGE, LANES), f32),
            pltpu.VMEM((3, EDGE + 2, EDGE + 2, EDGE, LANES), f32),
            pltpu.VMEM(((EDGE + 2) * EDGE * EDGE, 9 * LANES), bf16),
            pltpu.VMEM((16 * EDGE, LANES), f32),
        ],
        name="conv",
    )(rules[0], table, low, high, weights)
    coarser = shifted(pooled, "section", 1)
    order_out = send_order[0, 0].reshape(spaces, pair).T.reshape(-1)
    held = patch_order[0, 0]
    order_in = (held % pair) * spaces + held // pair
    slots, chosen = call(
        gather_kernel,
        (
            jax.ShapeDtypeStruct((tokens, LANES), f32),
            jax.ShapeDtypeStruct((tokens, 2 * LANES), bf16),
        ),
        [smem(), vmem()],
        name="gather",
    )(order_out, joined)
    message = call(
        join_kernel,
        (jax.ShapeDtypeStruct((packed_rows, LANES), bf16),),
        [vmem()] * 3,
        [pltpu.VMEM((tokens, LANES), f32), pltpu.VMEM((packed_rows, LANES), f32)],
        name="join",
    )(slots, chosen, coarser)[0]
    hidden = call(
        residual_kernel,
        (jax.ShapeDtypeStruct((96, tokens), bf16),),
        [vmem()] * 2,
        name="residual",
    )(joined, coarser)[0]
    inbound = exchange(message)

    def square(weight):
        return jnp.pad(weight[0], ((0, LANES - 96), (0, LANES - 96)))

    outbound = call(
        attend_kernel,
        (jax.ShapeDtypeStruct((packed_rows, LANES), bf16),),
        [smem()] + [vmem()] * 5,
        [
            pltpu.VMEM((packed_rows, LANES), f32),
            pltpu.VMEM((tokens, LANES), f32),
            pltpu.VMEM((tokens, LANES), f32),
            pltpu.VMEM((2, HEADS * PATCH, LANES), bf16),
            pltpu.VMEM((2, HEADS * PATCH, PATCH), f32),
            pltpu.VMEM((2, HEADS * PATCH, PATCH), bf16),
            pltpu.VMEM((2, 8, PATCH), f32),
            pltpu.VMEM((2, LANES, PATCH), f32),
        ],
        name="attend",
    )(
        order_in,
        inbound,
        jnp.pad(ln_gain.astype(f32), ((0, 0), (0, LANES - 96))),
        square(w_query),
        square(w_key),
        square(w_value),
    )[0]
    returned = exchange(outbound)
    result = call(
        finish_kernel,
        (jax.ShapeDtypeStruct((96, tokens), bf16),),
        [smem()] + [vmem()] * 4,
        [
            pltpu.VMEM((packed_rows, LANES), f32),
            pltpu.VMEM((tokens, LANES), f32),
            pltpu.VMEM((tokens, LANES), f32),
        ],
        name="finish",
    )(
        order_out,
        returned,
        hidden,
        mask,
        jnp.pad(w_out[0], ((0, 0), (0, LANES - 96))),
    )
    return result[0][None]


def solution(mesh):
    placed = (
        P("section", None, "space"),
        P("section", "space"),
        P("section", None, None, None),
        P("section", "space", None),
        P("section", "space", None, None),
        P("section", "space", None),
        P("section", "space", None),
        P("section", "space", None),
        P("section", None),
        P("section", None, None),
        P("section", None, None),
        P("section", None, None),
        P("section", None, None),
    )
    return jax.shard_map(
        shards, mesh=mesh, in_specs=placed, out_specs=P("section", None, "space"), check_vma=False
    )
```

```python
import functools
import math

import jax
import jax.numpy as jnp
from jax import lax
from jax.experimental import pallas as pl
from jax.experimental.pallas import tpu as pltpu
from jax.sharding import PartitionSpec as P

HEADS = 6
HEAD_DIM = 16
EDGE = 8
PATCH = 384
EPSILON = 1e-05
MASK_FILL = -1e30
LANES = 128
VOX = EDGE**3
ROWS = 10
CONTRACT_LAST = (((1,), (1,)), ((), ()))
VMEM_LIMIT = 24 << 20
FIRST_PEER = 80


def shifted(block, axis, distance):
    devices = range(lax.axis_size(axis))
    route = [(i - distance, i) for i in devices if i - distance in devices]
    return lax.ppermute(block, axis, route)


def swapped(block, axis, parity):
    count = lax.axis_size(axis)
    route = []
    for i in range(parity, count - 1, 2):
        route += [(i, i + 1), (i + 1, i)]
    return lax.ppermute(block, axis, route)


def vmem():
    return pl.BlockSpec(memory_space=pltpu.VMEM)


def smem():
    return pl.BlockSpec(memory_space=pltpu.SMEM)


def lane_of(shape):
    return lax.broadcasted_iota(jnp.int32, shape, len(shape) - 1)


def gather_rows(read_index, src, dst):
    for i in range(dst.shape[0]):
        dst[i : i + 1, :] = src[pl.ds(read_index(i), 1), :]


def scatter_rows(write_index, src, dst):
    for i in range(src.shape[0]):
        dst[pl.ds(write_index(i), 1), :] = src[i : i + 1, :]


def sent_token(order, first, peers):
    pair = order.shape[1] // peers
    return lambda i: order[0, (i % peers + first) % peers * pair + i // peers]


def pack_rows(slots, packed, with_mask):
    peers = slots.shape[0] // 12
    lane = lane_of((peers, LANES))
    tokens = [slots[t * peers : (t + 1) * peers, :] for t in range(12)]
    for group in range(3):
        extra = tokens[4 * group + 3]
        for j in range(3):
            row = jnp.where(
                lane < 96, tokens[4 * group + j], pltpu.roll(extra, 96 - 32 * j, axis=1)
            )
            packed[pl.ds(3 * group + j, peers, stride=ROWS), :] = row
    last = jnp.zeros((peers, LANES), jnp.float32)
    if with_mask:
        for t in range(12):
            last = jnp.where(lane == t, pltpu.roll(tokens[t], 32 + t, axis=1), last)
    packed[pl.ds(ROWS - 1, peers, stride=ROWS), :] = last


def unpack_rows(packed, slots, with_mask):
    peers = slots.shape[0] // 12
    lane = lane_of((peers, LANES))
    if with_mask:
        flags = packed[pl.ds(ROWS - 1, peers, stride=ROWS), :]
    for group in range(3):
        rows = [packed[pl.ds(3 * group + j, peers, stride=ROWS), :] for j in range(3)]
        extra = jnp.zeros((peers, LANES), jnp.float32)
        for j in range(3):
            spot = (lane >= 32 * j) & (lane < 32 * j + 32)
            extra = jnp.where(spot, pltpu.roll(rows[j], (32 * j + 32) % LANES, axis=1), extra)
        for j in range(4):
            t = 4 * group + j
            value = rows[j] if j < 3 else extra
            value = jnp.where(lane < 96, value, 0.0)
            if with_mask:
                value = jnp.where(lane == 96, pltpu.roll(flags, 96 - t, axis=1), value)
            slots[t * peers : (t + 1) * peers, :] = value


def send_kernel(lists, feats, mask, across, inside, slots, block, flags, ready):
    copies = [
        pltpu.make_async_copy(source, target, ready.at[i])
        for i, (source, target) in enumerate(((lists, slots), (feats, block), (mask, flags)))
    ]
    for copy in copies:
        copy.start()
    for copy in copies:
        copy.wait()
    odd = lax.rem(lax.axis_index("space"), 2)
    for out, row_index in ((across, odd), (inside, 1 - odd)):
        here = pl.ds(pl.multiple_of(slots[0, row_index] * VOX, VOX), VOX)
        shown = flags[:, here].astype(jnp.float32)
        out[...] = (block[:, here].astype(jnp.float32) * shown).astype(jnp.bfloat16)


def layout_kernel(octants, feats, mask, taps, table, weights):
    tokens = feats.shape[1]
    flags = mask[...].astype(jnp.float32)
    values = feats[...].astype(jnp.float32) * flags
    token = lax.broadcasted_iota(jnp.int32, (1, tokens), 1)
    x, y, z = (token >> 6) & 7, (token >> 3) & 7, token & 7
    octant = ((token >> 9) << 3) + ((x >> 2) << 2) + ((y >> 2) << 1) + (z >> 2)
    slot = jnp.full((1, tokens), 3, jnp.int32)
    for k in range(octants.shape[0] * 8):
        slot = jnp.where(octant == k, octants[k // 8, 0, k % 8], slot)
    within = ((x & 3) << 4) + ((y & 3) << 2) + (z & 3)
    child = jnp.where((slot < 3) & (mask[...] > 0), slot * 64 + within, 255).astype(jnp.float32)
    row = lax.broadcasted_iota(jnp.int32, (LANES - 96, tokens), 0)
    tail = jnp.where(row == 0, flags, jnp.where(row == 1, child, 0.0))
    table[...] = jnp.concatenate([values, tail], axis=0).T
    weights[...] = jnp.zeros(weights.shape, jnp.bfloat16)
    for k in range(27):
        at = (k % 9) * LANES
        weights[k // 9, 0:96, at : at + 96] = taps[k]


def conv_kernel(rules, own, across, inside, weights, joined, pooled, table, padded, views, halves):
    blocks = own.shape[0] // VOX
    pad_lanes = jnp.zeros((LANES - 96, VOX), jnp.float32)
    for b in range(blocks):
        table[b] = own[b * VOX : (b + 1) * VOX, :].reshape(EDGE, EDGE, EDGE, LANES)
    odd = lax.rem(lax.axis_index("space"), 2)
    for spot, ref in ((blocks + odd, across), (blocks + 1 - odd, inside)):
        values = jnp.concatenate([ref[...].astype(jnp.float32), pad_lanes], axis=0).T
        table[spot] = values.reshape(EDGE, EDGE, EDGE, LANES)
    table[blocks + 2] = jnp.zeros((EDGE, EDGE, EDGE, LANES), jnp.float32)

    def span(direction):
        if direction < 0:
            return pl.ds(EDGE - 1, 1), pl.ds(0, 1)
        if direction > 0:
            return pl.ds(0, 1), pl.ds(EDGE + 1, 1)
        return pl.ds(0, EDGE), pl.ds(1, EDGE)

    for b in range(blocks):

        def neighbor(dx, dy, dz):
            k = 9 * (dx + 1) + 3 * (dy + 1) + dz + 1
            if k == 13:
                return b
            return rules[b, 0, k if k < 13 else k - 1]

        for dx in (-1, 0, 1):
            sx, tx = span(dx)
            for dy in (-1, 0, 1):
                sy, ty = span(dy)
                here = table[neighbor(dx, dy, 0), sx, sy, :, :]
                below = table[neighbor(dx, dy, -1), sx, sy, :, :]
                above = table[neighbor(dx, dy, 1), sx, sy, :, :]
                z = lax.broadcasted_iota(jnp.int32, here.shape, 2)
                shape = here.shape
                flat = (shape[0] * shape[1] * EDGE, LANES)
                lower = jnp.where(z == EDGE - 1, below, here)
                upper = jnp.where(z == 0, above, here)
                padded[0, tx, ty, :, :] = pltpu.roll(lower, 1, axis=2)
                padded[1, tx, ty, :, :] = here
                padded[2, tx, ty, :, :] = pltpu.roll(upper, EDGE - 1, axis=2)
        for dy in range(3):
            for dz in range(3):
                k = dy * 3 + dz
                window = padded[dz, :, dy : dy + EDGE, :, :]
                views[:, k * LANES : (k + 1) * LANES] = window.reshape(
                    (EDGE + 2) * EDGE * EDGE, LANES
                ).astype(jnp.bfloat16)
        total = jnp.zeros((VOX, LANES), jnp.float32)
        for dx in range(3):
            total = total + lax.dot_general(
                views[dx * 64 : dx * 64 + VOX, :],
                weights[dx],
                CONTRACT_LAST,
                preferred_element_type=jnp.float32,
            )
        rows = own[b * VOX : (b + 1) * VOX, :]
        conv = total * rows[:, 96:97]
        joined[b * VOX : (b + 1) * VOX, :] = rows + conv
        quads = conv.reshape(4, 2, 4, 2, EDGE, LANES)
        summed = (quads[:, 0, :, 0] + quads[:, 0, :, 1]) + (quads[:, 1, :, 0] + quads[:, 1, :, 1])
        halves[...] = summed.reshape(16 * EDGE, LANES)
        even = halves[pl.ds(0, 64, stride=2), :]
        odd = halves[pl.ds(1, 64, stride=2), :]
        pooled[b * 64 : (b + 1) * 64, :] = ((even + odd) * 0.125).astype(jnp.bfloat16)


def child_matrix(rows):
    count = rows.shape[0]
    column = lax.broadcasted_iota(jnp.int32, (count, 2 * LANES), 1).astype(jnp.float32)
    return jnp.where(column == rows[:, 97:98], 1.0, 0.0).astype(jnp.bfloat16)


def lift(rows, chosen, coarser):
    blank = jnp.zeros((2 * LANES - coarser.shape[0], LANES), jnp.bfloat16)
    below = jnp.concatenate([coarser, blank], axis=0)
    return rows + jnp.dot(chosen, below, preferred_element_type=jnp.float32)


def gather_kernel(first, peers, order, joined, slots, chosen):
    gather_rows(sent_token(order, first, peers), joined, slots)
    chosen[...] = child_matrix(slots[...])


def join_kernel(slots, chosen, coarser, message, lifted, packed):
    lifted[...] = lift(slots[...], chosen[...], coarser[...])
    pack_rows(lifted, packed, True)
    message[...] = packed[...].astype(jnp.bfloat16)


def residual_kernel(joined, coarser, hidden):
    blocks = joined.shape[0] // VOX
    for b in range(blocks):
        rows = joined[b * VOX : (b + 1) * VOX, :]
        value = lift(rows, child_matrix(rows), coarser[...])
        hidden[:, b * VOX : (b + 1) * VOX] = value.T[:96].astype(jnp.bfloat16)


def attend_kernel(
    order, inbound, gain, w_query, w_key, w_value, outbound,
    packed, slots, rows, keys, scores, exponents, diagonal, attended,
):
    packed[...] = inbound[...].astype(jnp.float32)
    unpack_rows(packed, slots, True)
    gather_rows(lambda i: order[0, i], slots, rows)
    lane = lane_of((1, LANES))
    inside = lane < 96
    channel = lax.broadcasted_iota(jnp.int32, (LANES, PATCH), 0)
    factor = math.log2(math.e) / math.sqrt(HEAD_DIM)
    ones = jnp.ones((HEAD_DIM, PATCH), jnp.bfloat16)

    def project(left, right):
        return lax.dot_general(left, right, CONTRACT_LAST, preferred_element_type=jnp.float32)

    for patch in range(rows.shape[0] // PATCH):
        side = patch % 2
        serial = rows[patch * PATCH : (patch + 1) * PATCH, :]
        flags = serial[:, 96:97]
        values = jnp.where(inside, serial, 0.0)
        center = jnp.sum(values, axis=1, keepdims=True) * (1.0 / 96)
        spread = jnp.where(inside, values - center, 0.0)
        variance = jnp.sum(spread * spread, axis=1, keepdims=True) * (1.0 / 96)
        normed = (spread * lax.rsqrt(variance + EPSILON) * gain[...]).astype(jnp.bfloat16)
        query = project(w_query[...], normed) * factor
        query = jnp.where(channel == 96, 1.0, query).astype(jnp.bfloat16)
        keyed = project(normed, w_key[...])
        keyed = jnp.where(lane == 96, jnp.where(flags > 0, 0.0, MASK_FILL), keyed)
        keyed = keyed.astype(jnp.bfloat16)
        keyed_across = project(w_key[...], normed).astype(jnp.bfloat16)
        valued = project(w_value[...], normed).astype(jnp.bfloat16)
        products = query.astype(jnp.float32) * keyed_across.astype(jnp.float32)
        for head in range(HEADS):
            spot = (lane >= head * HEAD_DIM) & (lane < (head + 1) * HEAD_DIM) | (lane == 96)
            keys[side, head * PATCH : (head + 1) * PATCH, :] = keyed * jnp.where(
                spot, 1.0, 0.0
            ).astype(jnp.bfloat16)
        scores[side] = jnp.dot(keys[side], query, preferred_element_type=jnp.float32)
        alone = 1.0 - jnp.broadcast_to(flags, (PATCH, LANES)).T[0:1, :]
        for head in range(HEADS):
            group = slice(head * PATCH, (head + 1) * PATCH)
            channels = slice(head * HEAD_DIM, (head + 1) * HEAD_DIM)
            own = jnp.sum(products[channels], axis=0, keepdims=True)
            for part in range(PATCH // LANES):
                columns = slice(part * LANES, (part + 1) * LANES)
                here = scores[side, group, columns]
                top = jnp.maximum(jnp.max(here, axis=0, keepdims=True), own[:, columns])
                exponents[side, group, columns] = jnp.exp2(here - top).astype(jnp.bfloat16)
                extra = jnp.exp2(own[:, columns] - top) * alone[:, columns]
                diagonal[side, head : head + 1, columns] = extra
            left = jnp.concatenate([valued[channels], ones], axis=0)
            mixed = jnp.dot(left, exponents[side, group, :], preferred_element_type=jnp.float32)
            extra = diagonal[side, head : head + 1, :]
            upper = mixed[:HEAD_DIM] + extra * valued[channels].astype(jnp.float32)
            attended[side, channels, :] = upper / (mixed[HEAD_DIM : HEAD_DIM + 1] + extra)
        rows[patch * PATCH : (patch + 1) * PATCH, :] = attended[side].T
    scatter_rows(lambda i: order[0, i], rows, slots)
    pack_rows(slots, packed, False)
    outbound[...] = packed[...].astype(jnp.bfloat16)


def finish_kernel(first, peers, order, returned, hidden, mask, w_out, result, packed, slots, rows):
    packed[...] = returned[...].astype(jnp.float32)
    unpack_rows(packed, slots, False)
    scatter_rows(sent_token(order, first, peers), slots, rows)
    projected = lax.dot_general(
        w_out[...],
        rows[...].astype(jnp.bfloat16),
        (((1,), (1,)), ((), ())),
        preferred_element_type=jnp.float32,
    )
    value = hidden[...].astype(jnp.float32) + projected
    result[...] = (value * mask[...].astype(jnp.float32)).astype(jnp.bfloat16)


def call(body, outputs, in_specs, scratch=(), name=None):
    return pl.pallas_call(
        body,
        out_shape=outputs,
        in_specs=in_specs,
        out_specs=tuple(vmem() for _ in outputs),
        scratch_shapes=list(scratch),
        compiler_params=pltpu.CompilerParams(vmem_limit_bytes=VMEM_LIMIT),
        name=name,
    )


def exchange(packed, first):
    spaces = lax.axis_size("space")
    tiles = packed.reshape(packed.shape[0] // 2, 2, LANES)
    peers = [[(first + i) % spaces for i in range(spaces)]]
    return lax.all_to_all(
        tiles, "space", split_axis=0, concat_axis=0, axis_index_groups=peers, tiled=True
    ).reshape(packed.shape)


def shards(
    feats,
    mask,
    conv_w,
    rules,
    send_lists,
    pool_map,
    send_order,
    patch_order,
    ln_gain,
    w_query,
    w_key,
    w_value,
    w_out,
):
    f32, bf16 = jnp.float32, jnp.bfloat16
    tokens = feats.shape[2]
    blocks = tokens // VOX
    spaces = lax.axis_size("space")
    pair = tokens // spaces
    packed_rows = spaces * ROWS

    def in_hbm(array):
        return pltpu.with_memory_space_constraint(array, pltpu.HBM)

    across, inside = call(
        send_kernel,
        (jax.ShapeDtypeStruct((96, VOX), bf16),) * 2,
        [pl.BlockSpec(memory_space=pltpu.HBM)] * 3,
        [
            pltpu.SMEM((1, 2), jnp.int32),
            pltpu.VMEM((96, tokens), bf16),
            pltpu.VMEM((1, tokens), jnp.int32),
            pltpu.SemaphoreType.DMA((3,)),
        ],
        name="send",
    )(in_hbm(send_lists.reshape(1, 2)), in_hbm(feats[0]), in_hbm(mask))
    across = swapped(across, "space", 1)
    inside = swapped(inside, "space", 0)
    table, weights = call(
        layout_kernel,
        (
            jax.ShapeDtypeStruct((tokens, LANES), f32),
            jax.ShapeDtypeStruct((3, LANES, 9 * LANES), bf16),
        ),
        [smem()] + [vmem()] * 3,
        name="layout",
    )(pool_map.reshape(blocks, 1, 8), feats[0], mask, conv_w[0])
    joined, pooled = call(
        conv_kernel,
        (
            jax.ShapeDtypeStruct((tokens, LANES), f32),
            jax.ShapeDtypeStruct((blocks * 64, LANES), bf16),
        ),
        [smem()] + [vmem()] * 4,
        [
            pltpu.VMEM((blocks + 3, EDGE, EDGE, EDGE, LANES), f32),
            pltpu.VMEM((3, EDGE + 2, EDGE + 2, EDGE, LANES), f32),
            pltpu.VMEM(((EDGE + 2) * EDGE * EDGE, 9 * LANES), bf16),
            pltpu.VMEM((16 * EDGE, LANES), f32),
        ],
        name="conv",
    )(rules.reshape(blocks, 1, 26), table, across, inside, weights)
    coarser = shifted(pooled, "section", 1)
    first = FIRST_PEER % spaces
    order_out = send_order.reshape(1, tokens)
    held = patch_order.reshape(1, tokens)
    order_in = (held % pair) * spaces + (held // pair + (spaces - first)) % spaces
    slots, chosen = call(
        functools.partial(gather_kernel, first, spaces),
        (
            jax.ShapeDtypeStruct((tokens, LANES), f32),
            jax.ShapeDtypeStruct((tokens, 2 * LANES), bf16),
        ),
        [smem(), vmem()],
        name="gather",
    )(order_out, joined)
    message = call(
        join_kernel,
        (jax.ShapeDtypeStruct((packed_rows, LANES), bf16),),
        [vmem()] * 3,
        [pltpu.VMEM((tokens, LANES), f32), pltpu.VMEM((packed_rows, LANES), f32)],
        name="join",
    )(slots, chosen, coarser)[0]
    hidden = call(
        residual_kernel,
        (jax.ShapeDtypeStruct((96, tokens), bf16),),
        [vmem()] * 2,
        name="residual",
    )(joined, coarser)[0]
    inbound = exchange(message, first)

    def square(weight):
        return jnp.pad(weight[0], ((0, LANES - 96), (0, LANES - 96)))

    outbound = call(
        attend_kernel,
        (jax.ShapeDtypeStruct((packed_rows, LANES), bf16),),
        [smem()] + [vmem()] * 5,
        [
            pltpu.VMEM((packed_rows, LANES), f32),
            pltpu.VMEM((tokens, LANES), f32),
            pltpu.VMEM((tokens, LANES), f32),
            pltpu.VMEM((2, HEADS * PATCH, LANES), bf16),
            pltpu.VMEM((2, HEADS * PATCH, PATCH), f32),
            pltpu.VMEM((2, HEADS * PATCH, PATCH), bf16),
            pltpu.VMEM((2, 8, PATCH), f32),
            pltpu.VMEM((2, LANES, PATCH), f32),
        ],
        name="attend",
    )(
        order_in,
        inbound,
        jnp.pad(ln_gain.astype(f32), ((0, 0), (0, LANES - 96))),
        square(w_query),
        square(w_key),
        square(w_value),
    )[0]
    returned = exchange(outbound, first)
    result = call(
        functools.partial(finish_kernel, first, spaces),
        (jax.ShapeDtypeStruct((96, tokens), bf16),),
        [smem()] + [vmem()] * 4,
        [
            pltpu.VMEM((packed_rows, LANES), f32),
            pltpu.VMEM((tokens, LANES), f32),
            pltpu.VMEM((tokens, LANES), f32),
        ],
        name="finish",
    )(
        order_out,
        returned,
        hidden,
        mask,
        jnp.pad(w_out[0], ((0, 0), (0, LANES - 96))),
    )
    return result[0][None]


def solution(mesh):
    placed = (
        P("section", None, "space"),
        P("section", "space"),
        P("section", None, None, None),
        P("section", "space", None),
        P("section", "space", None, None),
        P("section", "space", None),
        P("section", "space", None),
        P("section", "space", None),
        P("section", None),
        P("section", None, None),
        P("section", None, None),
        P("section", None, None),
        P("section", None, None),
    )
    return jax.shard_map(
        shards, mesh=mesh, in_specs=placed, out_specs=P("section", None, "space"), check_vma=False
    )
```

```python
import functools
import math

import jax
import jax.numpy as jnp
from jax import lax
from jax.experimental import pallas as pl
from jax.experimental.pallas import tpu as pltpu
from jax.sharding import PartitionSpec as P

HEADS = 6
HEAD_DIM = 16
EDGE = 8
PATCH = 384
EPSILON = 1e-05
MASK_FILL = -1e30
LANES = 128
VOX = EDGE**3
ROWS = 10
CONTRACT_LAST = (((1,), (1,)), ((), ()))
VMEM_LIMIT = 24 << 20
FIRST_PEER = 80
RING = 16


def shifted(block, axis, distance):
    devices = range(lax.axis_size(axis))
    route = [(i - distance, i) for i in devices if i - distance in devices]
    return lax.ppermute(block, axis, route)


def swapped(block, axis, parity):
    count = lax.axis_size(axis)
    route = []
    for i in range(parity, count - 1, 2):
        route += [(i, i + 1), (i + 1, i)]
    return lax.ppermute(block, axis, route)


def vmem():
    return pl.BlockSpec(memory_space=pltpu.VMEM)


def smem():
    return pl.BlockSpec(memory_space=pltpu.SMEM)


def lane_of(shape):
    return lax.broadcasted_iota(jnp.int32, shape, len(shape) - 1)


def gather_rows(read_index, src, dst):
    for i in range(dst.shape[0]):
        dst[i : i + 1, :] = src[pl.ds(read_index(i), 1), :]


def scatter_rows(write_index, src, dst):
    for i in range(src.shape[0]):
        dst[pl.ds(write_index(i), 1), :] = src[i : i + 1, :]


def sent_token(order, peers):
    count = len(peers)
    pair = order.shape[1] // count
    return lambda i: order[0, peers[i % count] * pair + i // count]


def pack_rows(slots, packed, with_mask):
    peers = slots.shape[0] // 12
    lane = lane_of((peers, LANES))
    tokens = [slots[t * peers : (t + 1) * peers, :] for t in range(12)]
    for group in range(3):
        extra = tokens[4 * group + 3]
        for j in range(3):
            row = jnp.where(
                lane < 96, tokens[4 * group + j], pltpu.roll(extra, 96 - 32 * j, axis=1)
            )
            packed[pl.ds(3 * group + j, peers, stride=ROWS), :] = row
    last = jnp.zeros((peers, LANES), jnp.float32)
    if with_mask:
        for t in range(12):
            last = jnp.where(lane == t, pltpu.roll(tokens[t], 32 + t, axis=1), last)
    packed[pl.ds(ROWS - 1, peers, stride=ROWS), :] = last


def unpack_rows(packed, slots, with_mask):
    peers = slots.shape[0] // 12
    lane = lane_of((peers, LANES))
    if with_mask:
        flags = packed[pl.ds(ROWS - 1, peers, stride=ROWS), :]
    for group in range(3):
        rows = [packed[pl.ds(3 * group + j, peers, stride=ROWS), :] for j in range(3)]
        extra = jnp.zeros((peers, LANES), jnp.float32)
        for j in range(3):
            spot = (lane >= 32 * j) & (lane < 32 * j + 32)
            extra = jnp.where(spot, pltpu.roll(rows[j], (32 * j + 32) % LANES, axis=1), extra)
        for j in range(4):
            t = 4 * group + j
            value = rows[j] if j < 3 else extra
            value = jnp.where(lane < 96, value, 0.0)
            if with_mask:
                value = jnp.where(lane == 96, pltpu.roll(flags, 96 - t, axis=1), value)
            slots[t * peers : (t + 1) * peers, :] = value


def send_kernel(lists, feats, mask, across, inside, slots, block, flags, ready):
    copies = [
        pltpu.make_async_copy(source, target, ready.at[i])
        for i, (source, target) in enumerate(((lists, slots), (feats, block), (mask, flags)))
    ]
    for copy in copies:
        copy.start()
    for copy in copies:
        copy.wait()
    odd = lax.rem(lax.axis_index("space"), 2)
    for out, row_index in ((across, odd), (inside, 1 - odd)):
        here = pl.ds(pl.multiple_of(slots[0, row_index] * VOX, VOX), VOX)
        shown = flags[:, here].astype(jnp.float32)
        out[...] = (block[:, here].astype(jnp.float32) * shown).astype(jnp.bfloat16)


def layout_kernel(octants, feats, mask, source, table, weights, taps, ready):
    copy = pltpu.make_async_copy(source, taps, ready)
    copy.start()
    tokens = feats.shape[1]
    flags = mask[...].astype(jnp.float32)
    values = feats[...].astype(jnp.float32) * flags
    token = lax.broadcasted_iota(jnp.int32, (1, tokens), 1)
    x, y, z = (token >> 6) & 7, (token >> 3) & 7, token & 7
    octant = ((token >> 9) << 3) + ((x >> 2) << 2) + ((y >> 2) << 1) + (z >> 2)
    slot = jnp.full((1, tokens), 3, jnp.int32)
    for k in range(octants.shape[0] * 8):
        slot = jnp.where(octant == k, octants[k // 8, 0, k % 8], slot)
    within = ((x & 3) << 4) + ((y & 3) << 2) + (z & 3)
    child = jnp.where((slot < 3) & (mask[...] > 0), slot * 64 + within, 255).astype(jnp.float32)
    row = lax.broadcasted_iota(jnp.int32, (LANES - 96, tokens), 0)
    tail = jnp.where(row == 0, flags, jnp.where(row == 1, child, 0.0))
    table[...] = jnp.concatenate([values, tail], axis=0).T
    weights[...] = jnp.zeros(weights.shape, jnp.bfloat16)
    copy.wait()
    for k in range(27):
        at = (k % 9) * LANES
        down = (k // 9) * LANES
        weights[down : down + 96, at : at + 96] = taps[k]


def conv_kernel(
    source, own, across, inside, weights, joined, pooled, table, padded, views, halves, rules, ready
):
    copy = pltpu.make_async_copy(source, rules, ready)
    copy.start()
    blocks = own.shape[0] // VOX
    pad_lanes = jnp.zeros((LANES - 96, VOX), jnp.float32)
    for b in range(blocks):
        table[b] = own[b * VOX : (b + 1) * VOX, :].reshape(EDGE, EDGE, EDGE, LANES)
    odd = lax.rem(lax.axis_index("space"), 2)
    for spot, ref in ((blocks + odd, across), (blocks + 1 - odd, inside)):
        values = jnp.concatenate([ref[...].astype(jnp.float32), pad_lanes], axis=0).T
        table[spot] = values.reshape(EDGE, EDGE, EDGE, LANES)
    table[blocks + 2] = jnp.zeros((EDGE, EDGE, EDGE, LANES), jnp.float32)

    copy.wait()

    def span(direction):
        if direction < 0:
            return pl.ds(EDGE - 1, 1), pl.ds(0, 1)
        if direction > 0:
            return pl.ds(0, 1), pl.ds(EDGE + 1, 1)
        return pl.ds(0, EDGE), pl.ds(1, EDGE)

    for b in range(blocks):

        def neighbor(dx, dy, dz):
            k = 9 * (dx + 1) + 3 * (dy + 1) + dz + 1
            if k == 13:
                return b
            return rules[b, 0, k if k < 13 else k - 1]

        for dx in (-1, 0, 1):
            sx, tx = span(dx)
            for dy in (-1, 0, 1):
                sy, ty = span(dy)
                here = table[neighbor(dx, dy, 0), sx, sy, :, :]
                below = table[neighbor(dx, dy, -1), sx, sy, :, :]
                above = table[neighbor(dx, dy, 1), sx, sy, :, :]
                z = lax.broadcasted_iota(jnp.int32, here.shape, 2)
                shape = here.shape
                flat = (shape[0] * shape[1] * EDGE, LANES)
                lower = jnp.where(z == EDGE - 1, below, here)
                upper = jnp.where(z == 0, above, here)
                padded[0, tx, ty, :, :] = pltpu.roll(lower, 1, axis=2)
                padded[1, tx, ty, :, :] = here
                padded[2, tx, ty, :, :] = pltpu.roll(upper, EDGE - 1, axis=2)
        for dy in range(3):
            for dz in range(3):
                k = dy * 3 + dz
                window = padded[dz, :, dy : dy + EDGE, :, :]
                views[:, k * LANES : (k + 1) * LANES] = window.reshape(
                    (EDGE + 2) * EDGE * EDGE, LANES
                ).astype(jnp.bfloat16)
        first = lax.dot_general(
            views[0 : VOX + 64, :],
            weights[0 : 2 * LANES, :],
            CONTRACT_LAST,
            preferred_element_type=jnp.float32,
        )
        third = lax.dot_general(
            views[128 : VOX + 128, :],
            weights[2 * LANES :, :],
            CONTRACT_LAST,
            preferred_element_type=jnp.float32,
        )
        total = first[:VOX, :LANES] + first[64:, LANES:] + third
        rows = own[b * VOX : (b + 1) * VOX, :]
        conv = total * rows[:, 96:97]
        joined[b * VOX : (b + 1) * VOX, :] = rows + conv
        quads = conv.reshape(4, 2, 4, 2, EDGE, LANES)
        summed = (quads[:, 0, :, 0] + quads[:, 0, :, 1]) + (quads[:, 1, :, 0] + quads[:, 1, :, 1])
        halves[...] = summed.reshape(16 * EDGE, LANES)
        even = halves[pl.ds(0, 64, stride=2), :]
        odd = halves[pl.ds(1, 64, stride=2), :]
        pooled[b * 64 : (b + 1) * 64, :] = ((even + odd) * 0.125).astype(jnp.bfloat16)


def child_matrix(rows):
    count = rows.shape[0]
    column = lax.broadcasted_iota(jnp.int32, (count, 2 * LANES), 1).astype(jnp.float32)
    return jnp.where(column == rows[:, 97:98], 1.0, 0.0).astype(jnp.bfloat16)


def lift(rows, chosen, coarser):
    blank = jnp.zeros((2 * LANES - coarser.shape[0], LANES), jnp.bfloat16)
    below = jnp.concatenate([coarser, blank], axis=0)
    return rows + jnp.dot(chosen, below, preferred_element_type=jnp.float32)


def gather_kernel(peers, order, joined, slots, chosen):
    gather_rows(sent_token(order, peers), joined, slots)
    chosen[...] = child_matrix(slots[...])


def join_kernel(slots, chosen, coarser, message, lifted, packed):
    lifted[...] = lift(slots[...], chosen[...], coarser[...])
    pack_rows(lifted, packed, True)
    message[...] = packed[...].astype(jnp.bfloat16)


def residual_kernel(joined, coarser, hidden):
    blocks = joined.shape[0] // VOX
    for b in range(blocks):
        rows = joined[b * VOX : (b + 1) * VOX, :]
        value = lift(rows, child_matrix(rows), coarser[...])
        hidden[:, b * VOX : (b + 1) * VOX] = value.T[:96].astype(jnp.bfloat16)


def attend_kernel(
    order, inbound, gain, w_query, w_key, w_value, outbound,
    packed, slots, rows, keys, scores, exponents, diagonal, attended,
):
    packed[...] = inbound[...].astype(jnp.float32)
    unpack_rows(packed, slots, True)
    gather_rows(lambda i: order[0, i], slots, rows)
    lane = lane_of((1, LANES))
    inside = lane < 96
    channel = lax.broadcasted_iota(jnp.int32, (LANES, PATCH), 0)
    factor = math.log2(math.e) / math.sqrt(HEAD_DIM)
    ones = jnp.ones((HEAD_DIM, PATCH), jnp.bfloat16)

    def project(left, right):
        return lax.dot_general(left, right, CONTRACT_LAST, preferred_element_type=jnp.float32)

    for patch in range(rows.shape[0] // PATCH):
        side = patch % 2
        serial = rows[patch * PATCH : (patch + 1) * PATCH, :]
        flags = serial[:, 96:97]
        values = jnp.where(inside, serial, 0.0)
        center = jnp.sum(values, axis=1, keepdims=True) * (1.0 / 96)
        spread = jnp.where(inside, values - center, 0.0)
        variance = jnp.sum(spread * spread, axis=1, keepdims=True) * (1.0 / 96)
        normed = (spread * lax.rsqrt(variance + EPSILON) * gain[...]).astype(jnp.bfloat16)
        query = project(w_query[...], normed) * factor
        query = jnp.where(channel == 96, 1.0, query).astype(jnp.bfloat16)
        keyed = project(normed, w_key[...])
        keyed = jnp.where(lane == 96, jnp.where(flags > 0, 0.0, MASK_FILL), keyed)
        keyed = keyed.astype(jnp.bfloat16)
        keyed_across = project(w_key[...], normed).astype(jnp.bfloat16)
        valued = project(w_value[...], normed).astype(jnp.bfloat16)
        products = query.astype(jnp.float32) * keyed_across.astype(jnp.float32)
        for head in range(HEADS):
            spot = (lane >= head * HEAD_DIM) & (lane < (head + 1) * HEAD_DIM) | (lane == 96)
            keys[side, head * PATCH : (head + 1) * PATCH, :] = keyed * jnp.where(
                spot, 1.0, 0.0
            ).astype(jnp.bfloat16)
        scores[side] = jnp.dot(keys[side], query, preferred_element_type=jnp.float32)
        alone = 1.0 - jnp.broadcast_to(flags, (PATCH, LANES)).T[0:1, :]
        for head in range(HEADS):
            group = slice(head * PATCH, (head + 1) * PATCH)
            channels = slice(head * HEAD_DIM, (head + 1) * HEAD_DIM)
            own = jnp.sum(products[channels], axis=0, keepdims=True)
            for part in range(PATCH // LANES):
                columns = slice(part * LANES, (part + 1) * LANES)
                here = scores[side, group, columns]
                top = jnp.maximum(jnp.max(here, axis=0, keepdims=True), own[:, columns])
                exponents[side, group, columns] = jnp.exp2(here - top).astype(jnp.bfloat16)
                extra = jnp.exp2(own[:, columns] - top) * alone[:, columns]
                diagonal[side, head : head + 1, columns] = extra
            left = jnp.concatenate([valued[channels], ones], axis=0)
            mixed = jnp.dot(left, exponents[side, group, :], preferred_element_type=jnp.float32)
            extra = diagonal[side, head : head + 1, :]
            upper = mixed[:HEAD_DIM] + extra * valued[channels].astype(jnp.float32)
            attended[side, channels, :] = upper / (mixed[HEAD_DIM : HEAD_DIM + 1] + extra)
        rows[patch * PATCH : (patch + 1) * PATCH, :] = attended[side].T
    scatter_rows(lambda i: order[0, i], rows, slots)
    pack_rows(slots, packed, False)
    outbound[...] = packed[...].astype(jnp.bfloat16)


def finish_kernel(peers, order, returned, hidden, mask, w_out, result, packed, slots, rows):
    packed[...] = returned[...].astype(jnp.float32)
    unpack_rows(packed, slots, False)
    scatter_rows(sent_token(order, peers), slots, rows)
    projected = lax.dot_general(
        w_out[...],
        rows[...].astype(jnp.bfloat16),
        (((1,), (1,)), ((), ())),
        preferred_element_type=jnp.float32,
    )
    value = hidden[...].astype(jnp.float32) + projected
    result[...] = (value * mask[...].astype(jnp.float32)).astype(jnp.bfloat16)


def call(body, outputs, in_specs, scratch=(), name=None):
    return pl.pallas_call(
        body,
        out_shape=outputs,
        in_specs=in_specs,
        out_specs=tuple(vmem() for _ in outputs),
        scratch_shapes=list(scratch),
        compiler_params=pltpu.CompilerParams(vmem_limit_bytes=VMEM_LIMIT),
        name=name,
    )


def peer_order(spaces):
    first = FIRST_PEER % spaces

    def distance(i):
        y, z = i // (RING * 2), i // 2 % RING
        columns = max(spaces // (RING * 2), 1)
        return min(y, columns - y) + min(z, RING - z)

    return [first] + sorted(set(range(spaces)) - {first}, key=lambda i: (distance(i), i))


def exchange(packed, peers):
    tiles = packed.reshape(packed.shape[0] // 2, 2, LANES)
    return lax.all_to_all(
        tiles, "space", split_axis=0, concat_axis=0, axis_index_groups=[peers], tiled=True
    ).reshape(packed.shape)


def shards(
    feats,
    mask,
    conv_w,
    rules,
    send_lists,
    pool_map,
    send_order,
    patch_order,
    ln_gain,
    w_query,
    w_key,
    w_value,
    w_out,
):
    f32, bf16 = jnp.float32, jnp.bfloat16
    tokens = feats.shape[2]
    blocks = tokens // VOX
    spaces = lax.axis_size("space")
    pair = tokens // spaces
    packed_rows = spaces * ROWS

    def in_hbm(array):
        return pltpu.with_memory_space_constraint(array, pltpu.HBM)

    across, inside = call(
        send_kernel,
        (jax.ShapeDtypeStruct((96, VOX), bf16),) * 2,
        [pl.BlockSpec(memory_space=pltpu.HBM)] * 3,
        [
            pltpu.SMEM((1, 2), jnp.int32),
            pltpu.VMEM((96, tokens), bf16),
            pltpu.VMEM((1, tokens), jnp.int32),
            pltpu.SemaphoreType.DMA((3,)),
        ],
        name="send",
    )(in_hbm(send_lists.reshape(1, 2)), in_hbm(feats[0]), in_hbm(mask))
    across = swapped(across, "space", 1)
    inside = swapped(inside, "space", 0)
    table, weights = call(
        layout_kernel,
        (
            jax.ShapeDtypeStruct((tokens, LANES), f32),
            jax.ShapeDtypeStruct((3 * LANES, 9 * LANES), bf16),
        ),
        [smem()] + [vmem()] * 2 + [pl.BlockSpec(memory_space=pltpu.HBM)],
        [pltpu.VMEM((27, 96, 96), bf16), pltpu.SemaphoreType.DMA],
        name="layout",
    )(pool_map.reshape(blocks, 1, 8), feats[0], mask, in_hbm(conv_w[0]))
    joined, pooled = call(
        conv_kernel,
        (
            jax.ShapeDtypeStruct((tokens, LANES), f32),
            jax.ShapeDtypeStruct((blocks * 64, LANES), bf16),
        ),
        [pl.BlockSpec(memory_space=pltpu.HBM)] + [vmem()] * 4,
        [
            pltpu.VMEM((blocks + 3, EDGE, EDGE, EDGE, LANES), f32),
            pltpu.VMEM((3, EDGE + 2, EDGE + 2, EDGE, LANES), f32),
            pltpu.VMEM(((EDGE + 2) * EDGE * EDGE, 9 * LANES), bf16),
            pltpu.VMEM((16 * EDGE, LANES), f32),
            pltpu.SMEM((blocks, 1, 26), jnp.int32),
            pltpu.SemaphoreType.DMA,
        ],
        name="conv",
    )(in_hbm(rules.reshape(blocks, 1, 26)), table, across, inside, weights)
    coarser = shifted(pooled, "section", 1)
    peers = peer_order(spaces)
    order_out = send_order.reshape(1, tokens)
    held = patch_order.reshape(1, tokens)
    place = jnp.asarray([[peers.index(i) for i in range(spaces)]], bf16)
    match = (jnp.arange(spaces, dtype=jnp.int32)[:, None] == held // pair).astype(bf16)
    place = jnp.dot(place, match, preferred_element_type=f32).astype(jnp.int32)
    order_in = (held % pair) * spaces + place
    slots, chosen = call(
        functools.partial(gather_kernel, peers),
        (
            jax.ShapeDtypeStruct((tokens, LANES), f32),
            jax.ShapeDtypeStruct((tokens, 2 * LANES), bf16),
        ),
        [smem(), vmem()],
        name="gather",
    )(order_out, joined)
    message = call(
        join_kernel,
        (jax.ShapeDtypeStruct((packed_rows, LANES), bf16),),
        [vmem()] * 3,
        [pltpu.VMEM((tokens, LANES), f32), pltpu.VMEM((packed_rows, LANES), f32)],
        name="join",
    )(slots, chosen, coarser)[0]
    hidden = call(
        residual_kernel,
        (jax.ShapeDtypeStruct((96, tokens), bf16),),
        [vmem()] * 2,
        name="residual",
    )(joined, coarser)[0]
    inbound = exchange(message, peers)

    def square(weight):
        return jnp.pad(weight[0], ((0, LANES - 96), (0, LANES - 96)))

    outbound = call(
        attend_kernel,
        (jax.ShapeDtypeStruct((packed_rows, LANES), bf16),),
        [smem()] + [vmem()] * 5,
        [
            pltpu.VMEM((packed_rows, LANES), f32),
            pltpu.VMEM((tokens, LANES), f32),
            pltpu.VMEM((tokens, LANES), f32),
            pltpu.VMEM((2, HEADS * PATCH, LANES), bf16),
            pltpu.VMEM((2, HEADS * PATCH, PATCH), f32),
            pltpu.VMEM((2, HEADS * PATCH, PATCH), bf16),
            pltpu.VMEM((2, 8, PATCH), f32),
            pltpu.VMEM((2, LANES, PATCH), f32),
        ],
        name="attend",
    )(
        order_in,
        inbound,
        jnp.pad(ln_gain.astype(f32), ((0, 0), (0, LANES - 96))),
        square(w_query),
        square(w_key),
        square(w_value),
    )[0]
    returned = exchange(outbound, peers)
    result = call(
        functools.partial(finish_kernel, peers),
        (jax.ShapeDtypeStruct((96, tokens), bf16),),
        [smem()] + [vmem()] * 4,
        [
            pltpu.VMEM((packed_rows, LANES), f32),
            pltpu.VMEM((tokens, LANES), f32),
            pltpu.VMEM((tokens, LANES), f32),
        ],
        name="finish",
    )(
        order_out,
        returned,
        hidden,
        mask,
        jnp.pad(w_out[0], ((0, 0), (0, LANES - 96))),
    )
    return result[0][None]


def solution(mesh):
    placed = (
        P("section", None, "space"),
        P("section", "space"),
        P("section", None, None, None),
        P("section", "space", None),
        P("section", "space", None, None),
        P("section", "space", None),
        P("section", "space", None),
        P("section", "space", None),
        P("section", None),
        P("section", None, None),
        P("section", None, None),
        P("section", None, None),
        P("section", None, None),
    )
    return jax.shard_map(
        shards, mesh=mesh, in_specs=placed, out_specs=P("section", None, "space"), check_vma=False
    )
```

```python
import functools
import math

import jax
import jax.numpy as jnp
from jax import lax
from jax.experimental import pallas as pl
from jax.experimental.pallas import tpu as pltpu
from jax.sharding import PartitionSpec as P

HEADS = 6
HEAD_DIM = 16
EDGE = 8
PATCH = 384
EPSILON = 1e-05
MASK_FILL = -1e30
LANES = 128
VOX = EDGE**3
ROWS = 10
CONTRACT_LAST = (((1,), (1,)), ((), ()))
VMEM_LIMIT = 24 << 20
FIRST_PEER = 80
RING = 16


def shifted(block, axis, distance):
    devices = range(lax.axis_size(axis))
    route = [(i - distance, i) for i in devices if i - distance in devices]
    return lax.ppermute(block, axis, route)


def swapped(block, axis, parity):
    count = lax.axis_size(axis)
    route = []
    for i in range(parity, count - 1, 2):
        route += [(i, i + 1), (i + 1, i)]
    return lax.ppermute(block, axis, route)


def vmem():
    return pl.BlockSpec(memory_space=pltpu.VMEM)


def smem():
    return pl.BlockSpec(memory_space=pltpu.SMEM)


def lane_of(shape):
    return lax.broadcasted_iota(jnp.int32, shape, len(shape) - 1)


def gather_rows(read_index, src, dst):
    for i in range(dst.shape[0]):
        dst[i : i + 1, :] = src[pl.ds(read_index(i), 1), :]


def scatter_rows(write_index, src, dst):
    for i in range(src.shape[0]):
        dst[pl.ds(write_index(i), 1), :] = src[i : i + 1, :]


def sent_token(order, peers):
    count = len(peers)
    pair = order.shape[1] // count
    return lambda i: order[0, peers[i % count] * pair + i // count]


def pack_rows(slots, packed, with_mask):
    peers = slots.shape[0] // 12
    lane = lane_of((peers, LANES))
    tokens = [slots[t * peers : (t + 1) * peers, :] for t in range(12)]
    for group in range(3):
        extra = tokens[4 * group + 3]
        for j in range(3):
            row = jnp.where(
                lane < 96, tokens[4 * group + j], pltpu.roll(extra, 96 - 32 * j, axis=1)
            )
            packed[pl.ds(3 * group + j, peers, stride=ROWS), :] = row
    last = jnp.zeros((peers, LANES), jnp.float32)
    if with_mask:
        for t in range(12):
            last = jnp.where(lane == t, pltpu.roll(tokens[t], 32 + t, axis=1), last)
    packed[pl.ds(ROWS - 1, peers, stride=ROWS), :] = last


def unpack_rows(packed, slots, with_mask):
    peers = slots.shape[0] // 12
    lane = lane_of((peers, LANES))
    if with_mask:
        flags = packed[pl.ds(ROWS - 1, peers, stride=ROWS), :]
    for group in range(3):
        rows = [packed[pl.ds(3 * group + j, peers, stride=ROWS), :] for j in range(3)]
        extra = jnp.zeros((peers, LANES), jnp.float32)
        for j in range(3):
            spot = (lane >= 32 * j) & (lane < 32 * j + 32)
            extra = jnp.where(spot, pltpu.roll(rows[j], (32 * j + 32) % LANES, axis=1), extra)
        for j in range(4):
            t = 4 * group + j
            value = rows[j] if j < 3 else extra
            value = jnp.where(lane < 96, value, 0.0)
            if with_mask:
                value = jnp.where(lane == 96, pltpu.roll(flags, 96 - t, axis=1), value)
            slots[t * peers : (t + 1) * peers, :] = value


def send_kernel(
    lists, feats, mask, source, across, inside, taps, slots, block, flags, ready, later
):
    copies = [
        pltpu.make_async_copy(source, target, ready.at[i])
        for i, (source, target) in enumerate(((lists, slots), (feats, block), (mask, flags)))
    ]
    behind = pltpu.make_async_copy(source, taps, later)
    for copy in copies:
        copy.start()
    behind.start()
    for copy in copies:
        copy.wait()
    odd = lax.rem(lax.axis_index("space"), 2)
    for out, row_index in ((across, odd), (inside, 1 - odd)):
        here = pl.ds(pl.multiple_of(slots[0, row_index] * VOX, VOX), VOX)
        shown = flags[:, here].astype(jnp.float32)
        out[...] = (block[:, here].astype(jnp.float32) * shown).astype(jnp.bfloat16)
    behind.wait()


def layout_kernel(octants, feats, mask, taps, table, weights):
    tokens = feats.shape[1]
    flags = mask[...].astype(jnp.float32)
    values = feats[...].astype(jnp.float32) * flags
    token = lax.broadcasted_iota(jnp.int32, (1, tokens), 1)
    x, y, z = (token >> 6) & 7, (token >> 3) & 7, token & 7
    octant = ((token >> 9) << 3) + ((x >> 2) << 2) + ((y >> 2) << 1) + (z >> 2)
    slot = jnp.full((1, tokens), 3, jnp.int32)
    for k in range(octants.shape[0] * 8):
        slot = jnp.where(octant == k, octants[k // 8, 0, k % 8], slot)
    within = ((x & 3) << 4) + ((y & 3) << 2) + (z & 3)
    child = jnp.where((slot < 3) & (mask[...] > 0), slot * 64 + within, 255).astype(jnp.float32)
    row = lax.broadcasted_iota(jnp.int32, (LANES - 96, tokens), 0)
    tail = jnp.where(row == 0, flags, jnp.where(row == 1, child, 0.0))
    table[...] = jnp.concatenate([values, tail], axis=0).T
    weights[...] = jnp.zeros(weights.shape, jnp.bfloat16)
    for k in range(27):
        at = (k % 9) * LANES
        down = (k // 9) * LANES
        weights[down : down + 96, at : at + 96] = taps[k]


def conv_kernel(
    source, own, across, inside, weights, joined, pooled, table, padded, views, halves, rules, ready
):
    copy = pltpu.make_async_copy(source, rules, ready)
    copy.start()
    blocks = own.shape[0] // VOX
    pad_lanes = jnp.zeros((LANES - 96, VOX), jnp.float32)
    for b in range(blocks):
        table[b] = own[b * VOX : (b + 1) * VOX, :].reshape(EDGE, EDGE, EDGE, LANES)
    odd = lax.rem(lax.axis_index("space"), 2)
    for spot, ref in ((blocks + odd, across), (blocks + 1 - odd, inside)):
        values = jnp.concatenate([ref[...].astype(jnp.float32), pad_lanes], axis=0).T
        table[spot] = values.reshape(EDGE, EDGE, EDGE, LANES)
    table[blocks + 2] = jnp.zeros((EDGE, EDGE, EDGE, LANES), jnp.float32)

    copy.wait()

    def span(direction):
        if direction < 0:
            return pl.ds(EDGE - 1, 1), pl.ds(0, 1)
        if direction > 0:
            return pl.ds(0, 1), pl.ds(EDGE + 1, 1)
        return pl.ds(0, EDGE), pl.ds(1, EDGE)

    for b in range(blocks):

        def neighbor(dx, dy, dz):
            k = 9 * (dx + 1) + 3 * (dy + 1) + dz + 1
            if k == 13:
                return b
            return rules[b, 0, k if k < 13 else k - 1]

        for dx in (-1, 0, 1):
            sx, tx = span(dx)
            for dy in (-1, 0, 1):
                sy, ty = span(dy)
                here = table[neighbor(dx, dy, 0), sx, sy, :, :]
                below = table[neighbor(dx, dy, -1), sx, sy, :, :]
                above = table[neighbor(dx, dy, 1), sx, sy, :, :]
                z = lax.broadcasted_iota(jnp.int32, here.shape, 2)
                shape = here.shape
                flat = (shape[0] * shape[1] * EDGE, LANES)
                lower = jnp.where(z == EDGE - 1, below, here)
                upper = jnp.where(z == 0, above, here)
                padded[0, tx, ty, :, :] = pltpu.roll(lower, 1, axis=2)
                padded[1, tx, ty, :, :] = here
                padded[2, tx, ty, :, :] = pltpu.roll(upper, EDGE - 1, axis=2)
        for dy in range(3):
            for dz in range(3):
                k = dy * 3 + dz
                window = padded[dz, :, dy : dy + EDGE, :, :]
                views[:, k * LANES : (k + 1) * LANES] = window.reshape(
                    (EDGE + 2) * EDGE * EDGE, LANES
                ).astype(jnp.bfloat16)
        first = lax.dot_general(
            views[0 : VOX + 64, :],
            weights[0 : 2 * LANES, :],
            CONTRACT_LAST,
            preferred_element_type=jnp.float32,
        )
        third = lax.dot_general(
            views[128 : VOX + 128, :],
            weights[2 * LANES :, :],
            CONTRACT_LAST,
            preferred_element_type=jnp.float32,
        )
        total = first[:VOX, :LANES] + first[64:, LANES:] + third
        rows = own[b * VOX : (b + 1) * VOX, :]
        conv = total * rows[:, 96:97]
        joined[b * VOX : (b + 1) * VOX, :] = rows + conv
        quads = conv.reshape(4, 2, 4, 2, EDGE, LANES)
        summed = (quads[:, 0, :, 0] + quads[:, 0, :, 1]) + (quads[:, 1, :, 0] + quads[:, 1, :, 1])
        halves[...] = summed.reshape(16 * EDGE, LANES)
        even = halves[pl.ds(0, 64, stride=2), :]
        odd = halves[pl.ds(1, 64, stride=2), :]
        pooled[b * 64 : (b + 1) * 64, :] = ((even + odd) * 0.125).astype(jnp.bfloat16)


def child_matrix(rows):
    count = rows.shape[0]
    column = lax.broadcasted_iota(jnp.int32, (count, 2 * LANES), 1).astype(jnp.float32)
    return jnp.where(column == rows[:, 97:98], 1.0, 0.0).astype(jnp.bfloat16)


def lift(rows, chosen, coarser):
    blank = jnp.zeros((2 * LANES - coarser.shape[0], LANES), jnp.bfloat16)
    below = jnp.concatenate([coarser, blank], axis=0)
    return rows + jnp.dot(chosen, below, preferred_element_type=jnp.float32)


def gather_kernel(peers, order, joined, slots, chosen):
    gather_rows(sent_token(order, peers), joined, slots)
    chosen[...] = child_matrix(slots[...])


def join_kernel(slots, chosen, coarser, message, lifted, packed):
    lifted[...] = lift(slots[...], chosen[...], coarser[...])
    pack_rows(lifted, packed, True)
    message[...] = packed[...].astype(jnp.bfloat16)


def residual_kernel(joined, coarser, hidden):
    blocks = joined.shape[0] // VOX
    for b in range(blocks):
        rows = joined[b * VOX : (b + 1) * VOX, :]
        value = lift(rows, child_matrix(rows), coarser[...])
        hidden[:, b * VOX : (b + 1) * VOX] = value.T[:96].astype(jnp.bfloat16)


def attend_kernel(
    order, inbound, gain, w_query, w_key, w_value, outbound,
    packed, slots, rows, keys, scores, exponents, diagonal, attended,
):
    packed[...] = inbound[...].astype(jnp.float32)
    unpack_rows(packed, slots, True)
    gather_rows(lambda i: order[0, i], slots, rows)
    lane = lane_of((1, LANES))
    inside = lane < 96
    channel = lax.broadcasted_iota(jnp.int32, (LANES, PATCH), 0)
    factor = math.log2(math.e) / math.sqrt(HEAD_DIM)
    ones = jnp.ones((HEAD_DIM, PATCH), jnp.bfloat16)

    def project(left, right):
        return lax.dot_general(left, right, CONTRACT_LAST, preferred_element_type=jnp.float32)

    for patch in range(rows.shape[0] // PATCH):
        side = patch % 2
        serial = rows[patch * PATCH : (patch + 1) * PATCH, :]
        flags = serial[:, 96:97]
        values = jnp.where(inside, serial, 0.0)
        center = jnp.sum(values, axis=1, keepdims=True) * (1.0 / 96)
        spread = jnp.where(inside, values - center, 0.0)
        variance = jnp.sum(spread * spread, axis=1, keepdims=True) * (1.0 / 96)
        normed = (spread * lax.rsqrt(variance + EPSILON) * gain[...]).astype(jnp.bfloat16)
        query = project(w_query[...], normed) * factor
        query = jnp.where(channel == 96, 1.0, query).astype(jnp.bfloat16)
        keyed = project(normed, w_key[...])
        keyed = jnp.where(lane == 96, jnp.where(flags > 0, 0.0, MASK_FILL), keyed)
        keyed = keyed.astype(jnp.bfloat16)
        keyed_across = project(w_key[...], normed).astype(jnp.bfloat16)
        valued = project(w_value[...], normed).astype(jnp.bfloat16)
        products = query.astype(jnp.float32) * keyed_across.astype(jnp.float32)
        for head in range(HEADS):
            spot = (lane >= head * HEAD_DIM) & (lane < (head + 1) * HEAD_DIM) | (lane == 96)
            keys[side, head * PATCH : (head + 1) * PATCH, :] = keyed * jnp.where(
                spot, 1.0, 0.0
            ).astype(jnp.bfloat16)
        scores[side] = jnp.dot(keys[side], query, preferred_element_type=jnp.float32)
        alone = 1.0 - jnp.broadcast_to(flags, (PATCH, LANES)).T[0:1, :]
        for head in range(HEADS):
            group = slice(head * PATCH, (head + 1) * PATCH)
            channels = slice(head * HEAD_DIM, (head + 1) * HEAD_DIM)
            own = jnp.sum(products[channels], axis=0, keepdims=True)
            for part in range(PATCH // LANES):
                columns = slice(part * LANES, (part + 1) * LANES)
                here = scores[side, group, columns]
                top = jnp.maximum(jnp.max(here, axis=0, keepdims=True), own[:, columns])
                exponents[side, group, columns] = jnp.exp2(here - top).astype(jnp.bfloat16)
                extra = jnp.exp2(own[:, columns] - top) * alone[:, columns]
                diagonal[side, head : head + 1, columns] = extra
            left = jnp.concatenate([valued[channels], ones], axis=0)
            mixed = jnp.dot(left, exponents[side, group, :], preferred_element_type=jnp.float32)
            extra = diagonal[side, head : head + 1, :]
            upper = mixed[:HEAD_DIM] + extra * valued[channels].astype(jnp.float32)
            attended[side, channels, :] = upper / (mixed[HEAD_DIM : HEAD_DIM + 1] + extra)
        rows[patch * PATCH : (patch + 1) * PATCH, :] = attended[side].T
    scatter_rows(lambda i: order[0, i], rows, slots)
    pack_rows(slots, packed, False)
    outbound[...] = packed[...].astype(jnp.bfloat16)


def finish_kernel(peers, order, returned, hidden, mask, w_out, result, packed, slots, rows):
    packed[...] = returned[...].astype(jnp.float32)
    unpack_rows(packed, slots, False)
    scatter_rows(sent_token(order, peers), slots, rows)
    projected = lax.dot_general(
        w_out[...],
        rows[...].astype(jnp.bfloat16),
        (((1,), (1,)), ((), ())),
        preferred_element_type=jnp.float32,
    )
    value = hidden[...].astype(jnp.float32) + projected
    result[...] = (value * mask[...].astype(jnp.float32)).astype(jnp.bfloat16)


def call(body, outputs, in_specs, scratch=(), name=None):
    return pl.pallas_call(
        body,
        out_shape=outputs,
        in_specs=in_specs,
        out_specs=tuple(vmem() for _ in outputs),
        scratch_shapes=list(scratch),
        compiler_params=pltpu.CompilerParams(vmem_limit_bytes=VMEM_LIMIT),
        name=name,
    )


def peer_order(spaces):
    first = FIRST_PEER % spaces

    def distance(i):
        y, z = i // (RING * 2), i // 2 % RING
        columns = max(spaces // (RING * 2), 1)
        return min(y, columns - y) + min(z, RING - z)

    return [first] + sorted(set(range(spaces)) - {first}, key=lambda i: (distance(i), i))


def exchange(packed, peers):
    tiles = packed.reshape(packed.shape[0] // 2, 2, LANES)
    return lax.all_to_all(
        tiles, "space", split_axis=0, concat_axis=0, axis_index_groups=[peers], tiled=True
    ).reshape(packed.shape)


def shards(
    feats,
    mask,
    conv_w,
    rules,
    send_lists,
    pool_map,
    send_order,
    patch_order,
    ln_gain,
    w_query,
    w_key,
    w_value,
    w_out,
):
    f32, bf16 = jnp.float32, jnp.bfloat16
    tokens = feats.shape[2]
    blocks = tokens // VOX
    spaces = lax.axis_size("space")
    pair = tokens // spaces
    packed_rows = spaces * ROWS

    def in_hbm(array):
        return pltpu.with_memory_space_constraint(array, pltpu.HBM)

    across, inside, taps = call(
        send_kernel,
        (jax.ShapeDtypeStruct((96, VOX), bf16),) * 2 + (jax.ShapeDtypeStruct((27, 96, 96), bf16),),
        [pl.BlockSpec(memory_space=pltpu.HBM)] * 4,
        [
            pltpu.SMEM((1, 2), jnp.int32),
            pltpu.VMEM((96, tokens), bf16),
            pltpu.VMEM((1, tokens), jnp.int32),
            pltpu.SemaphoreType.DMA((3,)),
            pltpu.SemaphoreType.DMA,
        ],
        name="send",
    )(in_hbm(send_lists.reshape(1, 2)), in_hbm(feats[0]), in_hbm(mask), in_hbm(conv_w[0]))
    across = swapped(across, "space", 1)
    inside = swapped(inside, "space", 0)
    table, weights = call(
        layout_kernel,
        (
            jax.ShapeDtypeStruct((tokens, LANES), f32),
            jax.ShapeDtypeStruct((3 * LANES, 9 * LANES), bf16),
        ),
        [smem()] + [vmem()] * 3,
        name="layout",
    )(pool_map.reshape(blocks, 1, 8), feats[0], mask, taps)
    joined, pooled = call(
        conv_kernel,
        (
            jax.ShapeDtypeStruct((tokens, LANES), f32),
            jax.ShapeDtypeStruct((blocks * 64, LANES), bf16),
        ),
        [pl.BlockSpec(memory_space=pltpu.HBM)] + [vmem()] * 4,
        [
            pltpu.VMEM((blocks + 3, EDGE, EDGE, EDGE, LANES), f32),
            pltpu.VMEM((3, EDGE + 2, EDGE + 2, EDGE, LANES), f32),
            pltpu.VMEM(((EDGE + 2) * EDGE * EDGE, 9 * LANES), bf16),
            pltpu.VMEM((16 * EDGE, LANES), f32),
            pltpu.SMEM((blocks, 1, 26), jnp.int32),
            pltpu.SemaphoreType.DMA,
        ],
        name="conv",
    )(in_hbm(rules.reshape(blocks, 1, 26)), table, across, inside, weights)
    coarser = shifted(pooled, "section", 1)
    peers = peer_order(spaces)
    order_out = send_order.reshape(1, tokens)
    held = patch_order.reshape(1, tokens)
    place = jnp.asarray([[peers.index(i) for i in range(spaces)]], bf16)
    match = (jnp.arange(spaces, dtype=jnp.int32)[:, None] == held // pair).astype(bf16)
    place = jnp.dot(place, match, preferred_element_type=f32).astype(jnp.int32)
    order_in = (held % pair) * spaces + place
    slots, chosen = call(
        functools.partial(gather_kernel, peers),
        (
            jax.ShapeDtypeStruct((tokens, LANES), f32),
            jax.ShapeDtypeStruct((tokens, 2 * LANES), bf16),
        ),
        [smem(), vmem()],
        name="gather",
    )(order_out, joined)
    message = call(
        join_kernel,
        (jax.ShapeDtypeStruct((packed_rows, LANES), bf16),),
        [vmem()] * 3,
        [pltpu.VMEM((tokens, LANES), f32), pltpu.VMEM((packed_rows, LANES), f32)],
        name="join",
    )(slots, chosen, coarser)[0]
    hidden = call(
        residual_kernel,
        (jax.ShapeDtypeStruct((96, tokens), bf16),),
        [vmem()] * 2,
        name="residual",
    )(joined, coarser)[0]
    inbound = exchange(message, peers)

    def square(weight):
        return jnp.pad(weight[0], ((0, LANES - 96), (0, LANES - 96)))

    outbound = call(
        attend_kernel,
        (jax.ShapeDtypeStruct((packed_rows, LANES), bf16),),
        [smem()] + [vmem()] * 5,
        [
            pltpu.VMEM((packed_rows, LANES), f32),
            pltpu.VMEM((tokens, LANES), f32),
            pltpu.VMEM((tokens, LANES), f32),
            pltpu.VMEM((2, HEADS * PATCH, LANES), bf16),
            pltpu.VMEM((2, HEADS * PATCH, PATCH), f32),
            pltpu.VMEM((2, HEADS * PATCH, PATCH), bf16),
            pltpu.VMEM((2, 8, PATCH), f32),
            pltpu.VMEM((2, LANES, PATCH), f32),
        ],
        name="attend",
    )(
        order_in,
        inbound,
        jnp.pad(ln_gain.astype(f32), ((0, 0), (0, LANES - 96))),
        square(w_query),
        square(w_key),
        square(w_value),
    )[0]
    returned = exchange(outbound, peers)
    result = call(
        functools.partial(finish_kernel, peers),
        (jax.ShapeDtypeStruct((96, tokens), bf16),),
        [smem()] + [vmem()] * 4,
        [
            pltpu.VMEM((packed_rows, LANES), f32),
            pltpu.VMEM((tokens, LANES), f32),
            pltpu.VMEM((tokens, LANES), f32),
        ],
        name="finish",
    )(
        order_out,
        returned,
        hidden,
        mask,
        jnp.pad(w_out[0], ((0, 0), (0, LANES - 96))),
    )
    return result[0][None]


def solution(mesh):
    placed = (
        P("section", None, "space"),
        P("section", "space"),
        P("section", None, None, None),
        P("section", "space", None),
        P("section", "space", None, None),
        P("section", "space", None),
        P("section", "space", None),
        P("section", "space", None),
        P("section", None),
        P("section", None, None),
        P("section", None, None),
        P("section", None, None),
        P("section", None, None),
    )
    return jax.shard_map(
        shards, mesh=mesh, in_specs=placed, out_specs=P("section", None, "space"), check_vma=False
    )
```

```python
import functools
import math

import jax
import jax.numpy as jnp
from jax import lax
from jax.experimental import pallas as pl
from jax.experimental.pallas import tpu as pltpu
from jax.sharding import PartitionSpec as P

HEADS = 6
HEAD_DIM = 16
EDGE = 8
PATCH = 384
EPSILON = 1e-05
MASK_FILL = -1e30
LANES = 128
VOX = EDGE**3
ROWS = 10
CONTRACT_LAST = (((1,), (1,)), ((), ()))
VMEM_LIMIT = 24 << 20
FIRST_PEER = 112
RING = 16


def shifted(block, axis, distance):
    devices = range(lax.axis_size(axis))
    route = [(i - distance, i) for i in devices if i - distance in devices]
    return lax.ppermute(block, axis, route)


def swapped(block, axis, parity):
    count = lax.axis_size(axis)
    route = []
    for i in range(parity, count - 1, 2):
        route += [(i, i + 1), (i + 1, i)]
    return lax.ppermute(block, axis, route)


def vmem():
    return pl.BlockSpec(memory_space=pltpu.VMEM)


def smem():
    return pl.BlockSpec(memory_space=pltpu.SMEM)


def lane_of(shape):
    return lax.broadcasted_iota(jnp.int32, shape, len(shape) - 1)


def gather_rows(read_index, src, dst):
    for i in range(dst.shape[0]):
        dst[i : i + 1, :] = src[pl.ds(read_index(i), 1), :]


def scatter_rows(write_index, src, dst):
    for i in range(src.shape[0]):
        dst[pl.ds(write_index(i), 1), :] = src[i : i + 1, :]


def sent_token(order, peers):
    count = len(peers)
    pair = order.shape[1] // count
    return lambda i: order[0, peers[i % count] * pair + i // count]


def pack_rows(slots, packed, with_mask):
    peers = slots.shape[0] // 12
    lane = lane_of((peers, LANES))
    tokens = [slots[t * peers : (t + 1) * peers, :] for t in range(12)]
    for group in range(3):
        extra = tokens[4 * group + 3]
        for j in range(3):
            row = jnp.where(
                lane < 96, tokens[4 * group + j], pltpu.roll(extra, 96 - 32 * j, axis=1)
            )
            packed[pl.ds(3 * group + j, peers, stride=ROWS), :] = row
    last = jnp.zeros((peers, LANES), jnp.float32)
    if with_mask:
        for t in range(12):
            last = jnp.where(lane == t, pltpu.roll(tokens[t], 32 + t, axis=1), last)
    packed[pl.ds(ROWS - 1, peers, stride=ROWS), :] = last


def unpack_rows(packed, slots, with_mask):
    peers = slots.shape[0] // 12
    lane = lane_of((peers, LANES))
    if with_mask:
        flags = packed[pl.ds(ROWS - 1, peers, stride=ROWS), :]
    for group in range(3):
        rows = [packed[pl.ds(3 * group + j, peers, stride=ROWS), :] for j in range(3)]
        extra = jnp.zeros((peers, LANES), jnp.float32)
        for j in range(3):
            spot = (lane >= 32 * j) & (lane < 32 * j + 32)
            extra = jnp.where(spot, pltpu.roll(rows[j], (32 * j + 32) % LANES, axis=1), extra)
        for j in range(4):
            t = 4 * group + j
            value = rows[j] if j < 3 else extra
            value = jnp.where(lane < 96, value, 0.0)
            if with_mask:
                value = jnp.where(lane == 96, pltpu.roll(flags, 96 - t, axis=1), value)
            slots[t * peers : (t + 1) * peers, :] = value


def send_kernel(
    lists, feats, mask, source, across, inside, taps, slots, block, flags, ready, later
):
    copies = [
        pltpu.make_async_copy(source, target, ready.at[i])
        for i, (source, target) in enumerate(((lists, slots), (feats, block), (mask, flags)))
    ]
    behind = pltpu.make_async_copy(source, taps, later)
    for copy in copies:
        copy.start()
    behind.start()
    for copy in copies:
        copy.wait()
    odd = lax.rem(lax.axis_index("space"), 2)
    for out, row_index in ((across, odd), (inside, 1 - odd)):
        here = pl.ds(pl.multiple_of(slots[0, row_index] * VOX, VOX), VOX)
        shown = flags[:, here].astype(jnp.float32)
        out[...] = (block[:, here].astype(jnp.float32) * shown).astype(jnp.bfloat16)
    behind.wait()


def layout_kernel(octants, feats, mask, taps, table, weights):
    tokens = feats.shape[1]
    flags = mask[...].astype(jnp.float32)
    values = feats[...].astype(jnp.float32) * flags
    token = lax.broadcasted_iota(jnp.int32, (1, tokens), 1)
    x, y, z = (token >> 6) & 7, (token >> 3) & 7, token & 7
    octant = ((token >> 9) << 3) + ((x >> 2) << 2) + ((y >> 2) << 1) + (z >> 2)
    slot = jnp.full((1, tokens), 3, jnp.int32)
    for k in range(octants.shape[0] * 8):
        slot = jnp.where(octant == k, octants[k // 8, 0, k % 8], slot)
    within = ((x & 3) << 4) + ((y & 3) << 2) + (z & 3)
    child = jnp.where((slot < 3) & (mask[...] > 0), slot * 64 + within, 255).astype(jnp.float32)
    row = lax.broadcasted_iota(jnp.int32, (LANES - 96, tokens), 0)
    tail = jnp.where(row == 0, flags, jnp.where(row == 1, child, 0.0))
    table[...] = jnp.concatenate([values, tail], axis=0).T
    weights[...] = jnp.zeros(weights.shape, jnp.bfloat16)
    for k in range(27):
        at = (k % 9) * LANES
        down = (k // 9) * LANES
        weights[down : down + 96, at : at + 96] = taps[k]


def conv_kernel(
    source, own, across, inside, weights, joined, pooled, table, padded, views, halves, rules, ready
):
    copy = pltpu.make_async_copy(source, rules, ready)
    copy.start()
    blocks = own.shape[0] // VOX
    pad_lanes = jnp.zeros((LANES - 96, VOX), jnp.float32)
    for b in range(blocks):
        table[b] = own[b * VOX : (b + 1) * VOX, :].reshape(EDGE, EDGE, EDGE, LANES)
    odd = lax.rem(lax.axis_index("space"), 2)
    for spot, ref in ((blocks + odd, across), (blocks + 1 - odd, inside)):
        values = jnp.concatenate([ref[...].astype(jnp.float32), pad_lanes], axis=0).T
        table[spot] = values.reshape(EDGE, EDGE, EDGE, LANES)
    table[blocks + 2] = jnp.zeros((EDGE, EDGE, EDGE, LANES), jnp.float32)

    copy.wait()

    def span(direction):
        if direction < 0:
            return pl.ds(EDGE - 1, 1), pl.ds(0, 1)
        if direction > 0:
            return pl.ds(0, 1), pl.ds(EDGE + 1, 1)
        return pl.ds(0, EDGE), pl.ds(1, EDGE)

    for b in range(blocks):

        def neighbor(dx, dy, dz):
            k = 9 * (dx + 1) + 3 * (dy + 1) + dz + 1
            if k == 13:
                return b
            return rules[b, 0, k if k < 13 else k - 1]

        for dx in (-1, 0, 1):
            sx, tx = span(dx)
            for dy in (-1, 0, 1):
                sy, ty = span(dy)
                here = table[neighbor(dx, dy, 0), sx, sy, :, :]
                below = table[neighbor(dx, dy, -1), sx, sy, :, :]
                above = table[neighbor(dx, dy, 1), sx, sy, :, :]
                z = lax.broadcasted_iota(jnp.int32, here.shape, 2)
                shape = here.shape
                flat = (shape[0] * shape[1] * EDGE, LANES)
                lower = jnp.where(z == EDGE - 1, below, here)
                upper = jnp.where(z == 0, above, here)
                padded[0, tx, ty, :, :] = pltpu.roll(lower, 1, axis=2)
                padded[1, tx, ty, :, :] = here
                padded[2, tx, ty, :, :] = pltpu.roll(upper, EDGE - 1, axis=2)
        for dy in range(3):
            for dz in range(3):
                k = dy * 3 + dz
                window = padded[dz, :, dy : dy + EDGE, :, :]
                views[:, k * LANES : (k + 1) * LANES] = window.reshape(
                    (EDGE + 2) * EDGE * EDGE, LANES
                ).astype(jnp.bfloat16)
        first = lax.dot_general(
            views[0 : VOX + 64, :],
            weights[0 : 2 * LANES, :],
            CONTRACT_LAST,
            preferred_element_type=jnp.float32,
        )
        third = lax.dot_general(
            views[128 : VOX + 128, :],
            weights[2 * LANES :, :],
            CONTRACT_LAST,
            preferred_element_type=jnp.float32,
        )
        total = first[:VOX, :LANES] + first[64:, LANES:] + third
        rows = own[b * VOX : (b + 1) * VOX, :]
        conv = total * rows[:, 96:97]
        joined[b * VOX : (b + 1) * VOX, :] = rows + conv
        quads = conv.reshape(4, 2, 4, 2, EDGE, LANES)
        summed = (quads[:, 0, :, 0] + quads[:, 0, :, 1]) + (quads[:, 1, :, 0] + quads[:, 1, :, 1])
        halves[...] = summed.reshape(16 * EDGE, LANES)
        even = halves[pl.ds(0, 64, stride=2), :]
        odd = halves[pl.ds(1, 64, stride=2), :]
        pooled[b * 64 : (b + 1) * 64, :] = ((even + odd) * 0.125).astype(jnp.bfloat16)


def child_matrix(rows):
    count = rows.shape[0]
    column = lax.broadcasted_iota(jnp.int32, (count, 2 * LANES), 1).astype(jnp.float32)
    return jnp.where(column == rows[:, 97:98], 1.0, 0.0).astype(jnp.bfloat16)


def lift(rows, chosen, coarser):
    blank = jnp.zeros((2 * LANES - coarser.shape[0], LANES), jnp.bfloat16)
    below = jnp.concatenate([coarser, blank], axis=0)
    return rows + jnp.dot(chosen, below, preferred_element_type=jnp.float32)


def gather_kernel(peers, order, joined, slots, chosen):
    gather_rows(sent_token(order, peers), joined, slots)
    chosen[...] = child_matrix(slots[...])


def join_kernel(slots, chosen, coarser, message, lifted, packed):
    lifted[...] = lift(slots[...], chosen[...], coarser[...])
    pack_rows(lifted, packed, True)
    message[...] = packed[...].astype(jnp.bfloat16)


def residual_kernel(joined, coarser, hidden):
    blocks = joined.shape[0] // VOX
    for b in range(blocks):
        rows = joined[b * VOX : (b + 1) * VOX, :]
        value = lift(rows, child_matrix(rows), coarser[...])
        hidden[:, b * VOX : (b + 1) * VOX] = value.T[:96].astype(jnp.bfloat16)


def attend_kernel(
    order, inbound, gain, w_query, w_key, w_value, outbound,
    packed, slots, rows, keys, scores, exponents, diagonal, attended,
):
    packed[...] = inbound[...].astype(jnp.float32)
    unpack_rows(packed, slots, True)
    gather_rows(lambda i: order[0, i], slots, rows)
    lane = lane_of((1, LANES))
    inside = lane < 96
    channel = lax.broadcasted_iota(jnp.int32, (LANES, PATCH), 0)
    factor = math.log2(math.e) / math.sqrt(HEAD_DIM)
    ones = jnp.ones((HEAD_DIM, PATCH), jnp.bfloat16)

    def project(left, right):
        return lax.dot_general(left, right, CONTRACT_LAST, preferred_element_type=jnp.float32)

    for patch in range(rows.shape[0] // PATCH):
        side = patch % 2
        serial = rows[patch * PATCH : (patch + 1) * PATCH, :]
        flags = serial[:, 96:97]
        values = jnp.where(inside, serial, 0.0)
        center = jnp.sum(values, axis=1, keepdims=True) * (1.0 / 96)
        spread = jnp.where(inside, values - center, 0.0)
        variance = jnp.sum(spread * spread, axis=1, keepdims=True) * (1.0 / 96)
        normed = (spread * lax.rsqrt(variance + EPSILON) * gain[...]).astype(jnp.bfloat16)
        query = project(w_query[...], normed) * factor
        query = jnp.where(channel == 96, 1.0, query).astype(jnp.bfloat16)
        keyed = project(normed, w_key[...])
        keyed = jnp.where(lane == 96, jnp.where(flags > 0, 0.0, MASK_FILL), keyed)
        keyed = keyed.astype(jnp.bfloat16)
        keyed_across = project(w_key[...], normed).astype(jnp.bfloat16)
        valued = project(w_value[...], normed).astype(jnp.bfloat16)
        products = query.astype(jnp.float32) * keyed_across.astype(jnp.float32)
        for head in range(HEADS):
            spot = (lane >= head * HEAD_DIM) & (lane < (head + 1) * HEAD_DIM) | (lane == 96)
            keys[side, head * PATCH : (head + 1) * PATCH, :] = keyed * jnp.where(
                spot, 1.0, 0.0
            ).astype(jnp.bfloat16)
        scores[side] = jnp.dot(keys[side], query, preferred_element_type=jnp.float32)
        alone = 1.0 - jnp.broadcast_to(flags, (PATCH, LANES)).T[0:1, :]
        for head in range(HEADS):
            group = slice(head * PATCH, (head + 1) * PATCH)
            channels = slice(head * HEAD_DIM, (head + 1) * HEAD_DIM)
            own = jnp.sum(products[channels], axis=0, keepdims=True)
            for part in range(PATCH // LANES):
                columns = slice(part * LANES, (part + 1) * LANES)
                here = scores[side, group, columns]
                top = jnp.maximum(jnp.max(here, axis=0, keepdims=True), own[:, columns])
                exponents[side, group, columns] = jnp.exp2(here - top).astype(jnp.bfloat16)
                extra = jnp.exp2(own[:, columns] - top) * alone[:, columns]
                diagonal[side, head : head + 1, columns] = extra
            left = jnp.concatenate([valued[channels], ones], axis=0)
            mixed = jnp.dot(left, exponents[side, group, :], preferred_element_type=jnp.float32)
            extra = diagonal[side, head : head + 1, :]
            upper = mixed[:HEAD_DIM] + extra * valued[channels].astype(jnp.float32)
            attended[side, channels, :] = upper / (mixed[HEAD_DIM : HEAD_DIM + 1] + extra)
        rows[patch * PATCH : (patch + 1) * PATCH, :] = attended[side].T
    scatter_rows(lambda i: order[0, i], rows, slots)
    pack_rows(slots, packed, False)
    outbound[...] = packed[...].astype(jnp.bfloat16)


def finish_kernel(peers, order, returned, hidden, mask, w_out, result, packed, slots, rows):
    packed[...] = returned[...].astype(jnp.float32)
    unpack_rows(packed, slots, False)
    scatter_rows(sent_token(order, peers), slots, rows)
    projected = lax.dot_general(
        w_out[...],
        rows[...].astype(jnp.bfloat16),
        (((1,), (1,)), ((), ())),
        preferred_element_type=jnp.float32,
    )
    value = hidden[...].astype(jnp.float32) + projected
    result[...] = (value * mask[...].astype(jnp.float32)).astype(jnp.bfloat16)


def call(body, outputs, in_specs, scratch=(), name=None):
    return pl.pallas_call(
        body,
        out_shape=outputs,
        in_specs=in_specs,
        out_specs=tuple(vmem() for _ in outputs),
        scratch_shapes=list(scratch),
        compiler_params=pltpu.CompilerParams(vmem_limit_bytes=VMEM_LIMIT),
        name=name,
    )


def peer_order(spaces):
    first = FIRST_PEER % spaces

    def distance(i):
        y, z = i // (RING * 2), i // 2 % RING
        columns = max(spaces // (RING * 2), 1)
        return min(y, columns - y) + min(z, RING - z)

    return [first] + sorted(set(range(spaces)) - {first}, key=lambda i: (distance(i), i))


def exchange(packed, peers):
    tiles = packed.reshape(packed.shape[0] // 2, 2, LANES)
    return lax.all_to_all(
        tiles, "space", split_axis=0, concat_axis=0, axis_index_groups=[peers], tiled=True
    ).reshape(packed.shape)


def shards(
    feats,
    mask,
    conv_w,
    rules,
    send_lists,
    pool_map,
    send_order,
    patch_order,
    ln_gain,
    w_query,
    w_key,
    w_value,
    w_out,
):
    f32, bf16 = jnp.float32, jnp.bfloat16
    tokens = feats.shape[2]
    blocks = tokens // VOX
    spaces = lax.axis_size("space")
    pair = tokens // spaces
    packed_rows = spaces * ROWS

    def in_hbm(array):
        return pltpu.with_memory_space_constraint(array, pltpu.HBM)

    across, inside, taps = call(
        send_kernel,
        (jax.ShapeDtypeStruct((96, VOX), bf16),) * 2 + (jax.ShapeDtypeStruct((27, 96, 96), bf16),),
        [pl.BlockSpec(memory_space=pltpu.HBM)] * 4,
        [
            pltpu.SMEM((1, 2), jnp.int32),
            pltpu.VMEM((96, tokens), bf16),
            pltpu.VMEM((1, tokens), jnp.int32),
            pltpu.SemaphoreType.DMA((3,)),
            pltpu.SemaphoreType.DMA,
        ],
        name="send",
    )(in_hbm(send_lists.reshape(1, 2)), in_hbm(feats[0]), in_hbm(mask), in_hbm(conv_w[0]))
    across = swapped(across, "space", 1)
    inside = swapped(inside, "space", 0)
    table, weights = call(
        layout_kernel,
        (
            jax.ShapeDtypeStruct((tokens, LANES), f32),
            jax.ShapeDtypeStruct((3 * LANES, 9 * LANES), bf16),
        ),
        [smem()] + [vmem()] * 3,
        name="layout",
    )(pool_map.reshape(blocks, 1, 8), feats[0], mask, taps)
    joined, pooled = call(
        conv_kernel,
        (
            jax.ShapeDtypeStruct((tokens, LANES), f32),
            jax.ShapeDtypeStruct((blocks * 64, LANES), bf16),
        ),
        [pl.BlockSpec(memory_space=pltpu.HBM)] + [vmem()] * 4,
        [
            pltpu.VMEM((blocks + 3, EDGE, EDGE, EDGE, LANES), f32),
            pltpu.VMEM((3, EDGE + 2, EDGE + 2, EDGE, LANES), f32),
            pltpu.VMEM(((EDGE + 2) * EDGE * EDGE, 9 * LANES), bf16),
            pltpu.VMEM((16 * EDGE, LANES), f32),
            pltpu.SMEM((blocks, 1, 26), jnp.int32),
            pltpu.SemaphoreType.DMA,
        ],
        name="conv",
    )(in_hbm(rules.reshape(blocks, 1, 26)), table, across, inside, weights)
    coarser = shifted(pooled, "section", 1)
    peers = peer_order(spaces)
    order_out = send_order.reshape(1, tokens)
    held = patch_order.reshape(1, tokens)
    place = jnp.asarray([[peers.index(i) for i in range(spaces)]], bf16)
    match = (jnp.arange(spaces, dtype=jnp.int32)[:, None] == held // pair).astype(bf16)
    place = jnp.dot(place, match, preferred_element_type=f32).astype(jnp.int32)
    order_in = (held % pair) * spaces + place
    slots, chosen = call(
        functools.partial(gather_kernel, peers),
        (
            jax.ShapeDtypeStruct((tokens, LANES), f32),
            jax.ShapeDtypeStruct((tokens, 2 * LANES), bf16),
        ),
        [smem(), vmem()],
        name="gather",
    )(order_out, joined)
    message = call(
        join_kernel,
        (jax.ShapeDtypeStruct((packed_rows, LANES), bf16),),
        [vmem()] * 3,
        [pltpu.VMEM((tokens, LANES), f32), pltpu.VMEM((packed_rows, LANES), f32)],
        name="join",
    )(slots, chosen, coarser)[0]
    hidden = call(
        residual_kernel,
        (jax.ShapeDtypeStruct((96, tokens), bf16),),
        [vmem()] * 2,
        name="residual",
    )(joined, coarser)[0]
    inbound = exchange(message, peers)

    def square(weight):
        return jnp.pad(weight[0], ((0, LANES - 96), (0, LANES - 96)))

    outbound = call(
        attend_kernel,
        (jax.ShapeDtypeStruct((packed_rows, LANES), bf16),),
        [smem()] + [vmem()] * 5,
        [
            pltpu.VMEM((packed_rows, LANES), f32),
            pltpu.VMEM((tokens, LANES), f32),
            pltpu.VMEM((tokens, LANES), f32),
            pltpu.VMEM((2, HEADS * PATCH, LANES), bf16),
            pltpu.VMEM((2, HEADS * PATCH, PATCH), f32),
            pltpu.VMEM((2, HEADS * PATCH, PATCH), bf16),
            pltpu.VMEM((2, 8, PATCH), f32),
            pltpu.VMEM((2, LANES, PATCH), f32),
        ],
        name="attend",
    )(
        order_in,
        inbound,
        jnp.pad(ln_gain.astype(f32), ((0, 0), (0, LANES - 96))),
        square(w_query),
        square(w_key),
        square(w_value),
    )[0]
    returned = exchange(outbound, peers)
    result = call(
        functools.partial(finish_kernel, peers),
        (jax.ShapeDtypeStruct((96, tokens), bf16),),
        [smem()] + [vmem()] * 4,
        [
            pltpu.VMEM((packed_rows, LANES), f32),
            pltpu.VMEM((tokens, LANES), f32),
            pltpu.VMEM((tokens, LANES), f32),
        ],
        name="finish",
    )(
        order_out,
        returned,
        hidden,
        mask,
        jnp.pad(w_out[0], ((0, 0), (0, LANES - 96))),
    )
    return result[0][None]


def solution(mesh):
    placed = (
        P("section", None, "space"),
        P("section", "space"),
        P("section", None, None, None),
        P("section", "space", None),
        P("section", "space", None, None),
        P("section", "space", None),
        P("section", "space", None),
        P("section", "space", None),
        P("section", None),
        P("section", None, None),
        P("section", None, None),
        P("section", None, None),
        P("section", None, None),
    )
    return jax.shard_map(
        shards, mesh=mesh, in_specs=placed, out_specs=P("section", None, "space"), check_vma=False
    )
```
